32 devices in a mesh: pair: 4 (over y, core), fold: 8 (over z, x).
Axes of the slice: x: 2, y: 2, z: 4, core: 2. Of those that a mesh axis runs over, the one named last changes fastest.
Arguments:
- amplitudes: bfloat16 [4, 80, 640, 640], P(None, 'pair', 'fold'), may hold values from -6 to 6
- cycle_block: bfloat16 [640, 80, 8, 640], P('fold', None, 'pair'), may hold values from -0.078125 to 0.078125
- occ_sizes: int32 [8], replicated, may hold values from 1 to 20, 80 in all
- vir_sizes: int32 [8], replicated, may hold values from 1 to 160, 640 in all
- window_i: int32 [4], replicated, may hold values from 0 to 79
- window_occ: int32 [8], replicated, may hold values from 0 to 79
Outputs:
- residual: bfloat16 [4, 640, 8, 640], P(None, 'fold', 'pair')
The draws below stay inside these ranges and needn't reach their ends.
Inputs may be any that keep to these rules, and one draw needn't show every extreme that they name: `occ_sizes`: the entries sum to 80. `vir_sizes`: the entries sum to 640.
All inputs are finite; a program needn't handle non-finite values.
Results may differ from the reference program's by a relative error of at most 0.001.
Values may be sent and summed in bfloat16 or wider, within the bound.
A program may use at most 128 MiB of HBM per device.

```python
import math
import jax
import jax.numpy as jnp
import numpy as np
from jax import lax

V = 640
NK = 80
NI = 4
NJ = 8
IRREPS = 8


def with_ends(values, key, least, top_value):
    longest = values.shape.index(max(values.shape))
    spots = []
    for shift in (0, 1):
        where = [jax.random.randint(jax.random.fold_in(key, axis), (), 0, length) for axis, length in enumerate(values.shape)]
        where[longest] = (where[longest] + shift) % values.shape[longest]
        spots.append(tuple(where))
    return values.at[spots[0]].set(least).at[spots[1]].set(top_value)


def spiked(array, stream_key, source, target, blocks, factor):
    def block_of(dim):
        return (jnp.arange(array.shape[dim]) // (array.shape[dim] // blocks)).reshape((-1,) + (1,) * (array.ndim - 1 - dim))

    first = jax.random.permutation(stream_key, blocks)[block_of(target)]
    other_side = (block_of(target) + blocks // 2) % blocks
    return jnp.where((block_of(source) == first) | (block_of(source) == other_side), factor * array, array)


def shard_levels(own_key, shape, pieces, least, top_value):
    def one(position, parts):
        steps = jax.random.uniform(jax.random.fold_in(jax.random.fold_in(own_key, 6), position), (parts,), jnp.float32, least / len(pieces), top_value / len(pieces))
        return jnp.repeat(jnp.exp(steps), shape[position] // parts).reshape((-1,) + (1,) * (len(shape) - position - 1))

    factor_of = one(*pieces[0])
    for cut in pieces[1:]:
        factor_of = factor_of * one(*cut)
    return factor_of


def length_profile(amount, total, bound, slope):
    loads = [(1 << 20) // math.isqrt(grade ** slope) + 1 for grade in range(2, amount + 1)]
    spare, counts = total - bound - (amount - 1), [1] * (amount - 1)
    while spare > 0:
        free = [i for i in range(amount - 1) if counts[i] < bound]
        whole, remaining = sum([loads[i] for i in free]), spare
        for i in free:
            extra = min(bound - counts[i], max(1, remaining * loads[i] // whole), spare)
            counts[i] = counts[i] + extra
            spare = spare - extra
    return np.array([bound] + counts)


def uneven(rng, amount, total, limit, slope):
    if amount == 2:
        one = jax.random.randint(rng, (), max(1, total - limit), min(limit, total - 1) + 1)
        return jnp.stack([one, total - one])
    tallies = jnp.asarray(length_profile(amount, total, limit, slope), jnp.int32)
    pairs = (amount - 1) // 2
    giver, sink = tallies[1:1 + 2 * pairs:2], tallies[2:2 + 2 * pairs:2]
    slack = jnp.minimum(giver - 1, limit - sink)
    shifted = jax.random.randint(jax.random.fold_in(rng, 1), (pairs,), 0, 1 << 20) % (slack + 1)
    tallies = tallies.at[1:1 + 2 * pairs:2].set(giver - shifted).at[2:2 + 2 * pairs:2].set(sink + shifted)
    return tallies[jax.random.permutation(jax.random.fold_in(rng, 2), amount)]


def centred(own_key, dims, width, most, shards=(), kind=jnp.bfloat16):
    values = width * jax.random.normal(own_key, dims, jnp.float32)
    if shards:
        values = values * shard_levels(own_key, dims, shards, -0.22, 0.18)
    return jnp.clip(values, -most, most).astype(kind)


def noise_with(key, shape, deviation, reach, cuts, heavy, kind=jnp.bfloat16):
    drawn = deviation * jax.random.normal(key, shape, jnp.float32)
    if cuts:
        drawn = drawn * shard_levels(key, shape, cuts, -0.22, 0.18)
    return jnp.clip(spiked(drawn, jax.random.fold_in(key, 3), *heavy), -reach, reach).astype(kind)


def setup_inputs(seed: int = 0) -> dict:
    key_of = jax.random.split(jax.random.key(seed), 7)
    amplitudes = noise_with(key_of[0], (NI, NK, V, V), 1.0, 6.0, ((1, 4), (2, 8)), (3, 2, 8, 2.0))
    cycle_block = centred(key_of[1], (V, NK, NJ, V), (NK * V // 8) ** -0.5, 0.078125, ((0, 8), (2, 4)))
    occ_sizes = uneven(key_of[2], IRREPS, NK, NK // 4, 2).astype(jnp.int32)
    vir_sizes = uneven(key_of[3], IRREPS, V, V // 4, 2).astype(jnp.int32)
    window_i = with_ends(jax.random.randint(key_of[4], (NI,), 0, NK), jax.random.fold_in(key_of[4], 1), 0, NK - 1).astype(jnp.int32)
    window_occ = with_ends(jax.random.randint(key_of[5], (NJ,), 0, NK), jax.random.fold_in(key_of[5], 1), 0, NK - 1).astype(jnp.int32)
    return dict(amplitudes=amplitudes, cycle_block=cycle_block, occ_sizes=occ_sizes, vir_sizes=vir_sizes, window_i=window_i, window_occ=window_occ)


def irrep_labels(sizes, count):
    boundaries = jnp.cumsum(sizes).astype(jnp.int32)
    positions = jnp.arange(count, dtype=jnp.int32)
    return jnp.sum((positions[:, None] >= boundaries[None, :]).astype(jnp.int32), axis=1).astype(jnp.int32)


def reference(amplitudes, cycle_block, occ_sizes, vir_sizes, window_i, window_occ):
    occ_labels = irrep_labels(occ_sizes, NK)
    vir_labels = irrep_labels(vir_sizes, V)
    i_labels = occ_labels[window_i]
    amp_parity = jnp.bitwise_xor(
        jnp.bitwise_xor(i_labels[:, None, None, None], occ_labels[None, :, None, None]),
        jnp.bitwise_xor(vir_labels[None, None, :, None], vir_labels[None, None, None, :]))
    masked_amps = jnp.where(amp_parity == 0, amplitudes, jnp.zeros_like(amplitudes))
    left_matrix = jnp.transpose(masked_amps, (0, 2, 1, 3)).reshape(NI * V, NK * V)

    def one_column(column):
        column_slab = lax.dynamic_index_in_dim(cycle_block, column, 2, keepdims=False)
        j_label = occ_labels[window_occ[column]]
        parity = jnp.bitwise_xor(jnp.bitwise_xor(vir_labels[:, None, None], occ_labels[None, :, None]), jnp.bitwise_xor(j_label, vir_labels[None, None, :]))
        masked = jnp.where(parity == 0, column_slab, jnp.zeros_like(column_slab))
        right_matrix = jnp.transpose(masked, (1, 0, 2)).reshape(NK * V, V)
        return jnp.dot(left_matrix, right_matrix, preferred_element_type=jnp.float32).astype(jnp.bfloat16)

    results = lax.map(one_column, jnp.arange(NJ, dtype=jnp.int32))
    return jnp.transpose(results.reshape(NJ, NI, V, V), (1, 2, 0, 3))
```

```python
import functools

import jax
import jax.numpy as jnp
from jax import lax
from jax.experimental import pallas as pl
from jax.experimental.pallas import tpu as pltpu
from jax.sharding import PartitionSpec as P

LANES = 128
FOLDS = 4
STEPS = 32000.0
FINE = 8.0


def irrep_labels(sizes, count):
    boundaries = jnp.cumsum(sizes)
    positions = jnp.arange(count, dtype=jnp.int32)
    return jnp.sum((positions[:, None] >= boundaries[None, :]).astype(jnp.int32), axis=1)


def label_lookup(orbitals, labels, count):
    matches = orbitals[:, None] == jnp.arange(count, dtype=jnp.int32)[None, :]
    return jnp.sum(jnp.where(matches, labels[None, :], 0), axis=1)


def narrow(labels):
    return labels.astype(jnp.float32).astype(jnp.bfloat16)


def fold_columns(values, rows, lanes):
    v_pack = values.shape[1] // FOLDS
    total = jnp.zeros((values.shape[0], v_pack), values.dtype)
    for q in range(FOLDS):
        cut = slice(q * v_pack, (q + 1) * v_pack)
        total = jnp.where(rows == lanes[:, cut], values[:, cut], total)
    return total


def pack_t_kernel(label_ref, row_ref, vir_ref, t_ref, out_ref):
    piece = pl.program_id(0)
    k_local = t_ref.shape[1]
    rest = t_ref.shape[-1] // FOLDS - LANES
    group = LANES // rest
    tails = []
    for k in range(k_local):
        lanes = narrow(vir_ref[...] ^ label_ref[piece * k_local + k])
        total = fold_columns(t_ref[0, k, 0], row_ref[0], lanes)
        out_ref[0, k] = total[:, :LANES]
        tails.append(total[:, LANES:])
        if k == k_local - 1:
            tails += [jnp.zeros_like(tails[0])] * (group - len(tails))
        if len(tails) == group:
            out_ref[0, k_local + k // group] = jnp.concatenate(tails, axis=1)
            tails = []


def pack_t(amplitudes, ik_labels, a_labels, vir_labels, n_pair):
    n_i, k_local, a_rows, vir_total = amplitudes.shape
    split = n_pair // n_i
    rows = a_rows // split
    rest = vir_total // FOLDS - LANES
    depth = k_local + -(-k_local * rest // LANES)
    source = amplitudes.reshape(n_i, k_local, split, rows, vir_total)
    labels = jnp.broadcast_to(ik_labels[:, None, :], (n_i, split, k_local)).reshape(-1)
    return pl.pallas_call(
        pack_t_kernel,
        grid=(n_pair,),
        out_shape=jax.ShapeDtypeStruct((n_pair, depth, rows, LANES), amplitudes.dtype),
        in_specs=[
            pl.BlockSpec(memory_space=pltpu.SMEM),
            pl.BlockSpec((1, rows, 1), lambda p: (p % split, 0, 0)),
            pl.BlockSpec((1, vir_total), lambda p: (0, 0)),
            pl.BlockSpec((1, k_local, 1, rows, vir_total), lambda p: (p // split, 0, p % split, 0, 0)),
        ],
        out_specs=pl.BlockSpec((1, depth, rows, LANES), lambda p: (p, 0, 0, 0)),
        compiler_params=pltpu.CompilerParams(vmem_limit_bytes=32 << 20),
    )(labels, narrow(a_labels).reshape(split, rows, 1), vir_labels[None, :], source)


def pack_w_kernel(occ_ref, row_ref, vir_ref, w_ref, out_ref, main_ref, rest_ref):
    block = pl.program_id(0)
    c_local, ks, j_local, vir_total = w_ref.shape
    rest = vir_total // FOLDS - LANES
    for k in range(ks):
        lanes = narrow(vir_ref[...] ^ occ_ref[block * ks + k])
        values = w_ref[:, k].reshape(c_local * j_local, vir_total)
        total = fold_columns(values, row_ref[...], lanes).astype(jnp.float32)
        main_ref[...] = total[:, :LANES]
        rest_ref[:, :rest] = total[:, LANES:]
        for j in range(j_local):
            own = pl.ds(j, c_local, stride=j_local)
            out_ref[j, k * c_local:(k + 1) * c_local, :LANES] = main_ref[own, :].astype(out_ref.dtype)
            out_ref[j, k * c_local:(k + 1) * c_local, LANES:] = rest_ref[own, :][:, :rest].astype(out_ref.dtype)


def pack_w(cycle_block, occ_labels, cj_labels, vir_labels):
    c_local, occ_total, j_local, vir_total = cycle_block.shape
    v_pack = vir_total // FOLDS
    ks = 8
    return pl.pallas_call(
        pack_w_kernel,
        grid=(occ_total // ks,),
        out_shape=jax.ShapeDtypeStruct((j_local, occ_total * c_local, v_pack), cycle_block.dtype),
        in_specs=[
            pl.BlockSpec(memory_space=pltpu.SMEM),
            pl.BlockSpec((c_local * j_local, 1), lambda k: (0, 0)),
            pl.BlockSpec((1, vir_total), lambda k: (0, 0)),
            pl.BlockSpec((c_local, ks, j_local, vir_total), lambda k: (0, k, 0, 0)),
        ],
        out_specs=pl.BlockSpec((j_local, ks * c_local, v_pack), lambda k: (0, k, 0)),
        scratch_shapes=[pltpu.VMEM((c_local * j_local, LANES), jnp.float32)] * 2,
        compiler_params=pltpu.CompilerParams(vmem_limit_bytes=32 << 20),
        cost_estimate=pl.CostEstimate(
            flops=0, bytes_accessed=4 * cycle_block.size, transcendentals=0
        ),
    )(occ_labels, narrow(cj_labels).reshape(-1, 1), vir_labels[None, :], cycle_block)


def flip(index, bits, count):
    total, bit = 0, 1
    while bit < count:
        total = total + (index // bit + bits // bit) % 2 * bit
        bit *= 2
    return total


def encode(parts, out_ref):
    top = functools.reduce(jnp.maximum, [jnp.max(jnp.abs(part), axis=1, keepdims=True) for part in parts])
    code = jnp.ceil(jnp.log2(jnp.maximum(top, 1e-30)) * FINE)
    factor = STEPS * jnp.exp2(code * (-1.0 / FINE))
    scaled = [jnp.round(part * factor).astype(jnp.int32) for part in parts]
    rest = [part[:, LANES:] for part in scaled]
    spare = LANES - sum(part.shape[1] for part in rest)
    rest.append(jnp.broadcast_to(code.astype(jnp.int32), (code.shape[0], spare)))
    for j, part in enumerate(scaled):
        out_ref[:, j * LANES:(j + 1) * LANES] = part[:, :LANES].astype(jnp.int16)
    out_ref[:, len(parts) * LANES:] = jnp.concatenate(rest, axis=1).astype(jnp.int16)


def decode(packed, count, width):
    values = packed.astype(jnp.int32).astype(jnp.float32)
    code = values[:, -1:]
    values = values * (jnp.exp2(code * (1.0 / FINE)) / STEPS)
    rest = width - LANES
    return [
        jnp.concatenate(
            [
                values[:, j * LANES:(j + 1) * LANES],
                values[:, count * LANES + j * rest:count * LANES + (j + 1) * rest],
            ],
            axis=1,
        )
        for j in range(count)
    ]


def contract_kernel(
    n_pair, n_fold, occ_ref, own_ref, vir_ref, row_ref, col_ref, moved_ref, w_ref, out_ref,
    wide, held, total, x_out, x_in, z_out, z_in,
    copy_sem, f_send, f_recv, y_send, y_recv, c_send, c_recv, x_send, x_recv, z_send, z_recv,
):
    pair, fold = lax.axis_index("pair"), lax.axis_index("fold")
    n_y, n_outer, here = n_pair // 2, n_fold // 2, n_fold // FOLDS
    y, core = pair // 2, pair % 2
    outer, half = fold // 2, fold % 2
    mate = y * 2 + 1 - core
    rows, v_pack = own_ref.shape[0], vir_ref.shape[2]
    k_local = moved_ref.shape[1] - -(-moved_ref.shape[1] * (v_pack - LANES) // v_pack)
    k_pack = occ_ref.shape[0] // FOLDS
    c_local = v_pack // here
    depth = k_pack * c_local
    rest = v_pack - LANES
    group = LANES // rest
    j_local = w_ref.shape[0]

    barrier = pltpu.get_barrier_semaphore()
    for step in range(1, n_fold):
        pl.semaphore_signal(barrier, device_id={"fold": (fold + step) % n_fold})
    for step in range(1, n_y):
        pl.semaphore_signal(barrier, device_id={"pair": (y + step) % n_y * 2 + core})
    pl.semaphore_signal(barrier, device_id={"pair": mate})
    pl.semaphore_wait(barrier, n_fold + n_y - 1)

    def to_fold(target):
        return pltpu.make_async_remote_copy(
            src_ref=wide.at[target], dst_ref=held.at[fold, pair],
            send_sem=f_send.at[target], recv_sem=f_recv.at[fold], device_id={"fold": target},
        )

    def from_fold(source):
        return pltpu.make_async_remote_copy(
            src_ref=wide.at[source], dst_ref=held.at[source, pair],
            send_sem=f_send.at[source], recv_sem=f_recv.at[source], device_id={"fold": source},
        )

    def over_y(source, step):
        other = (y + step) % n_y
        return pltpu.make_async_remote_copy(
            src_ref=held.at[source, pair], dst_ref=held.at[source, pair],
            send_sem=y_send.at[source, other], recv_sem=y_recv.at[source, y],
            device_id={"pair": other * 2 + core},
        )

    def from_y(source, step):
        other = (y + step) % n_y
        slot = held.at[source, other * 2 + core]
        return pltpu.make_async_remote_copy(
            src_ref=slot, dst_ref=slot,
            send_sem=y_send.at[source, other], recv_sem=y_recv.at[source, other],
            device_id={"pair": other * 2 + core},
        )

    def over_core(source, step):
        other = (y + step) % n_y
        slot = held.at[source, other * 2 + core]
        return pltpu.make_async_remote_copy(
            src_ref=slot, dst_ref=slot,
            send_sem=c_send.at[source, other], recv_sem=c_recv.at[source, other],
            device_id={"pair": mate},
        )

    def from_core(source, step):
        other = (y + step) % n_y
        slot = held.at[source, other * 2 + 1 - core]
        return pltpu.make_async_remote_copy(
            src_ref=slot, dst_ref=slot,
            send_sem=c_send.at[source, other], recv_sem=c_recv.at[source, other],
            device_id={"pair": mate},
        )

    def over_x(block):
        return pltpu.make_async_remote_copy(
            src_ref=x_out.at[block], dst_ref=x_in.at[block],
            send_sem=x_send.at[block], recv_sem=x_recv.at[block],
            device_id={"fold": outer * 2 + 1 - half},
        )

    def over_z(block, slot):
        return pltpu.make_async_remote_copy(
            src_ref=z_out.at[block], dst_ref=z_in.at[slot],
            send_sem=z_send.at[block], recv_sem=z_recv.at[slot],
            device_id={"fold": block * 2 + half},
        )

    def own_copy():
        return pltpu.make_async_copy(wide.at[fold], held.at[fold, pair], copy_sem)

    def quarter(step, carry):
        q = flip(fold // here, step, FOLDS)
        labels = narrow(own_ref[...] ^ vir_ref[q])
        pieces = [[] for _ in range(here)]
        for kappa in range(k_pack):
            chosen = jnp.zeros((rows, v_pack), moved_ref.dtype)
            for s in range(FOLDS):
                k = s * k_pack + kappa
                side, inner = k // k_local, k % k_local
                tail = inner % group * rest
                piece = jnp.concatenate(
                    [
                        moved_ref[side, inner],
                        moved_ref[side, k_local + inner // group][:, tail:tail + rest],
                    ],
                    axis=1,
                )
                chosen = jnp.where(labels == occ_ref[k], piece, chosen)
            for f in range(here):
                pieces[f].append(chosen[:, f * c_local:(f + 1) * c_local])
        for f in range(here):
            spare = wide.shape[2] - depth
            if spare:
                pieces[f].append(jnp.zeros((rows, spare), moved_ref.dtype))
            target = q * here + f
            wide[target] = jnp.concatenate(pieces[f], axis=1)
        for f in range(here):
            target = q * here + f

            @pl.when(step * here + f > 0)
            def _():
                other = q * here + (fold + f) % here
                to_fold(other).start()

        return carry

    lax.fori_loop(0, FOLDS, quarter, 0)
    own_copy().start()
    own_copy().wait()

    def source_of(step):
        return flip(outer, step // 2, n_outer) * 2 + (half + 1 + step) % 2

    def relay(source):
        for step in range(1, n_y):
            over_y(source, step).start()
        over_core(source, 0).start()

    def pass_on(source):
        for step in range(1, n_y):
            from_y(source, step).wait_recv()
            over_core(source, step).start()

    relay(fold)
    first = source_of(0)
    from_fold(first).wait_recv()
    relay(first)
    pass_on(first)

    def contract(step, carry):
        source = source_of(step)

        @pl.when(step + 2 < n_fold)
        def _():
            later = source_of(step + 2)
            from_fold(later).wait_recv()
            relay(later)

        @pl.when(step + 1 < n_fold)
        def _():
            pass_on(source_of(step + 1))

        for other in range(n_y):
            from_core(source, other).wait_recv()
        left = jnp.concatenate([held[source, p][:, :depth] for p in range(n_pair)], axis=0)
        labels = row_ref[source]
        parts = [None] * j_local
        for s in range(FOLDS):
            part = jnp.where(labels == col_ref[s], left, jnp.zeros_like(left))
            for j in range(j_local):
                term = jnp.dot(
                    part, w_ref[j, s * depth:(s + 1) * depth], preferred_element_type=jnp.float32
                )
                parts[j] = term if s == 0 else parts[j] + term
        block = flip(outer, step // 2, n_outer)
        for j in range(j_local):
            total[j] = parts[j]

        @pl.when(step % 2 == 0)
        def _():
            encode([total[j] for j in range(j_local)], x_out.at[block])
            over_x(block).start()

        @pl.when(step % 2 == 1)
        def _():
            over_x(block).wait_recv()
            near = decode(x_in[block], j_local, v_pack)
            near = [total[j] + near[j] for j in range(j_local)]

            @pl.when(step == 1)
            def _():
                for j in range(j_local):
                    out_ref[j] = near[j]

            @pl.when(step > 1)
            def _():
                encode(near, z_out.at[block])
                over_z(block, outer).start()

        return carry

    lax.fori_loop(0, n_fold, contract, 0)

    def finish(step, carry):
        block = flip(outer, step, n_outer)
        over_z(block, block).wait_recv()
        far = decode(z_in[block], j_local, v_pack)
        for j in range(j_local):
            out_ref[j] += far[j]
        return carry

    lax.fori_loop(1, n_outer, finish, 0)

    def drain(source, carry):
        @pl.when(source != fold)
        def _():
            to_fold(source).wait_send()

        for step in range(1, n_y):
            over_y(source, step).wait_send()
        for step in range(n_y):
            over_core(source, step).wait_send()
        return carry

    lax.fori_loop(0, n_fold, drain, 0)

    def drain_sums(block, carry):
        over_x(block).wait_send()

        @pl.when(block != outer)
        def _():
            over_z(block, outer).wait_send()

        return carry

    lax.fori_loop(0, n_outer, drain_sums, 0)


def contract_all(n_pair, n_fold, moved, packed_w, occ_labels, own_labels, vir_labels, row_labels, col_labels):
    _, _, rows, _ = moved.shape
    j_local, _, v_pack = packed_w.shape
    depth = col_labels.shape[-1]
    wide = -(-depth // LANES) * LANES
    n_y, n_outer = n_pair // 2, n_fold // 2
    count = n_pair * rows
    lanes = (j_local + -(-(j_local * (v_pack - LANES) + 1) // LANES)) * LANES
    occ = jnp.broadcast_to(narrow(occ_labels)[:, None, None], (occ_labels.shape[0], 1, v_pack))
    sems = pltpu.SemaphoreType.DMA
    vmem = pl.BlockSpec(memory_space=pltpu.VMEM)
    return pl.pallas_call(
        functools.partial(contract_kernel, n_pair, n_fold),
        out_shape=jax.ShapeDtypeStruct((j_local, count, v_pack), jnp.float32),
        in_specs=[vmem] * 7,
        out_specs=vmem,
        scratch_shapes=[
            pltpu.VMEM((n_fold, rows, wide), moved.dtype),
            pltpu.VMEM((n_fold, n_pair, rows, wide), moved.dtype),
            pltpu.VMEM((j_local, count, v_pack), jnp.float32),
        ]
        + [pltpu.VMEM((n_outer, count, lanes), jnp.int16)] * 4
        + [
            sems, sems((n_fold,)), sems((n_fold,)), sems((n_fold, n_y)), sems((n_fold, n_y)),
            sems((n_fold, n_y)), sems((n_fold, n_y)),
            sems((n_outer,)), sems((n_outer,)), sems((n_outer,)), sems((n_outer,)),
        ],
        compiler_params=pltpu.CompilerParams(
            collective_id=0, has_side_effects=True, vmem_limit_bytes=56 << 20
        ),
    )(occ, own_labels[:, None], vir_labels.reshape(FOLDS, 1, v_pack), narrow(row_labels), narrow(col_labels), moved, packed_w)


def body(n_pair, n_fold, amplitudes, cycle_block, occ_sizes, vir_sizes, window_i, window_occ):
    c_local, occ_total, j_local, vir_total = cycle_block.shape
    n_i, k_local, a_rows, _ = amplitudes.shape
    v_pack = vir_total // FOLDS
    k_pack = occ_total // FOLDS
    rows = n_i * a_rows // n_pair
    fold = lax.axis_index("fold")
    pair = lax.axis_index("pair")
    occ_labels = irrep_labels(occ_sizes, occ_total)
    vir_labels = irrep_labels(vir_sizes, vir_total)
    c_labels = lax.dynamic_slice_in_dim(vir_labels, fold * c_local, c_local)
    a_labels = lax.dynamic_slice_in_dim(vir_labels, fold * a_rows, a_rows)
    k_labels = lax.dynamic_slice_in_dim(occ_labels, pair * k_local, k_local)
    i_labels = label_lookup(window_i, occ_labels, occ_total)
    j_orbitals = lax.dynamic_slice_in_dim(window_occ, pair * j_local, j_local)
    j_labels = label_lookup(j_orbitals, occ_labels, occ_total)

    parts = pack_t(amplitudes, i_labels[:, None] ^ k_labels[None, :], a_labels, vir_labels, n_pair)
    moved = lax.all_to_all(parts, "pair", split_axis=0, concat_axis=0, tiled=True)
    packed_w = pack_w(cycle_block, occ_labels, c_labels[:, None] ^ j_labels[None, :], vir_labels)

    ia_labels = (i_labels[:, None] ^ a_labels[None, :]).reshape(n_pair, rows)
    own_labels = lax.dynamic_slice_in_dim(ia_labels, pair, 1)[0]
    row_labels = (vir_labels.reshape(n_fold, 1, a_rows) ^ i_labels[None, :, None]).reshape(n_fold, -1, 1)
    col_labels = (occ_labels[:, None] ^ c_labels[None, :]).reshape(FOLDS, 1, k_pack * c_local)
    summed = contract_all(
        n_pair, n_fold, moved, packed_w, occ_labels, own_labels, vir_labels, row_labels, col_labels
    )
    own = summed.astype(jnp.bfloat16).reshape(j_local, n_i, a_rows, v_pack).transpose(1, 2, 0, 3)
    iaj = i_labels[:, None, None] ^ a_labels[None, :, None] ^ j_labels[None, None, :]
    keep = iaj[..., None] == vir_labels
    return jnp.where(keep, jnp.concatenate([own] * FOLDS, axis=-1), 0)


def solution(mesh):
    sizes = mesh.shape["pair"], mesh.shape["fold"]
    placed = (P(None, "pair", "fold", None), P("fold", None, "pair", None), P(), P(), P(), P())

    def run(*args):
        return body(*sizes, *args)

    return jax.shard_map(
        run, mesh=mesh, in_specs=placed, out_specs=P(None, "fold", "pair", None), check_vma=False
    )
```

```python
import functools
import math

import jax
import jax.numpy as jnp
from jax import lax
from jax.experimental import pallas as pl
from jax.experimental.pallas import tpu as pltpu
from jax.sharding import PartitionSpec as P

LANES = 128
FOLDS = 4
AHEAD = 3
STEPS = 32000.0
FINE = 8.0


def irrep_labels(sizes, count):
    boundaries = jnp.cumsum(sizes)
    positions = jnp.arange(count, dtype=jnp.int32)
    return jnp.sum((positions[:, None] >= boundaries[None, :]).astype(jnp.int32), axis=1)


def label_lookup(orbitals, labels, count):
    matches = orbitals[:, None] == jnp.arange(count, dtype=jnp.int32)[None, :]
    return jnp.sum(jnp.where(matches, labels[None, :], 0), axis=1)


def narrow(labels):
    return labels.astype(jnp.float32).astype(jnp.bfloat16)


def fold_columns(values, rows, lanes):
    v_pack = values.shape[1] // FOLDS
    total = jnp.zeros((values.shape[0], v_pack), values.dtype)
    for q in range(FOLDS):
        cut = slice(q * v_pack, (q + 1) * v_pack)
        total = jnp.where(rows == lanes[:, cut], values[:, cut], total)
    return total


def pack_t_kernel(label_ref, row_ref, vir_ref, t_ref, out_ref):
    piece = pl.program_id(0)
    k_local = t_ref.shape[1]
    rest = t_ref.shape[-1] // FOLDS - LANES
    group = LANES // rest
    tails = []
    for k in range(k_local):
        lanes = narrow(vir_ref[...] ^ label_ref[piece * k_local + k])
        total = fold_columns(t_ref[0, k, 0], row_ref[0], lanes)
        base = k // group * (group + 1)
        out_ref[0, base + k % group] = total[:, :LANES]
        tails.append(total[:, LANES:])
        if k == k_local - 1:
            tails += [jnp.zeros_like(tails[0])] * (group - len(tails))
        if len(tails) == group:
            out_ref[0, base + group] = jnp.concatenate(tails, axis=1)
            tails = []


def pack_t(amplitudes, ik_labels, a_labels, vir_labels, n_pair):
    n_i, k_local, a_rows, vir_total = amplitudes.shape
    split = n_pair // n_i
    rows = a_rows // split
    group = LANES // (vir_total // FOLDS - LANES)
    slabs = -(-k_local // group) * (group + 1)
    source = amplitudes.reshape(n_i, k_local, split, rows, vir_total)
    labels = jnp.broadcast_to(ik_labels[:, None, :], (n_i, split, k_local)).reshape(-1)
    return pl.pallas_call(
        pack_t_kernel,
        grid=(n_pair,),
        out_shape=jax.ShapeDtypeStruct((n_pair, slabs, rows, LANES), amplitudes.dtype),
        in_specs=[
            pl.BlockSpec(memory_space=pltpu.SMEM),
            pl.BlockSpec((1, rows, 1), lambda p: (p % split, 0, 0)),
            pl.BlockSpec((1, vir_total), lambda p: (0, 0)),
            pl.BlockSpec((1, k_local, 1, rows, vir_total), lambda p: (p // split, 0, p % split, 0, 0)),
        ],
        out_specs=pl.BlockSpec((1, slabs, rows, LANES), lambda p: (p, 0, 0, 0)),
        compiler_params=pltpu.CompilerParams(vmem_limit_bytes=32 << 20),
    )(labels, narrow(a_labels).reshape(split, rows, 1), vir_labels[None, :], source)


def flip(index, bits, count):
    total, bit = 0, 1
    while bit < count:
        total = total + (index // bit + bits // bit) % 2 * bit
        bit *= 2
    return total


def encode(parts, out_ref):
    top = functools.reduce(jnp.maximum, [jnp.max(jnp.abs(part), axis=1, keepdims=True) for part in parts])
    code = jnp.ceil(jnp.log2(jnp.maximum(top, 1e-30)) * FINE)
    factor = STEPS * jnp.exp2(code * (-1.0 / FINE))
    scaled = [jnp.round(part * factor).astype(jnp.int32) for part in parts]
    rest = [part[:, LANES:] for part in scaled]
    spare = LANES - sum(part.shape[1] for part in rest)
    rest.append(jnp.broadcast_to(code.astype(jnp.int32), (code.shape[0], spare)))
    for j, part in enumerate(scaled):
        out_ref[:, j * LANES:(j + 1) * LANES] = part[:, :LANES].astype(jnp.int16)
    out_ref[:, len(parts) * LANES:] = jnp.concatenate(rest, axis=1).astype(jnp.int16)


def decode(packed, count, width):
    values = packed.astype(jnp.int32).astype(jnp.float32)
    code = values[:, -1:]
    values = values * (jnp.exp2(code * (1.0 / FINE)) / STEPS)
    rest = width - LANES
    return [
        jnp.concatenate(
            [
                values[:, j * LANES:(j + 1) * LANES],
                values[:, count * LANES + j * rest:count * LANES + (j + 1) * rest],
            ],
            axis=1,
        )
        for j in range(count)
    ]


def spans_of(k_pack, c_local):
    step = LANES // math.gcd(LANES, c_local)
    return [(0, step), (step, k_pack - step)]


def cycle_kernel(
    n_pair, n_fold, label_ref, occ_ref, own_ref, vir_ref, line_ref, cj_ref, row_ref, col_ref, parts_ref, w_hbm,
    out_ref, moved, wide, held, packed_w, raw_w, main_w, rest_w, total, x_out, x_in, z_out, z_in,
    copy_sem, w_sem, a_send, a_recv, f_send, f_recv, y_send, y_recv, c_send, c_recv,
    x_send, x_recv, z_send, z_recv,
):
    pair, fold = lax.axis_index("pair"), lax.axis_index("fold")
    n_y, n_outer, here = n_pair // 2, n_fold // 2, n_fold // FOLDS
    y, core = pair // 2, pair % 2
    outer, half = fold // 2, fold % 2
    mate = y * 2 + 1 - core
    rows, v_pack = own_ref.shape[0], vir_ref.shape[2]
    c_local, occ_total, j_local, vir_total = w_hbm.shape
    k_pack, k_local = occ_total // FOLDS, occ_total // n_pair
    rest = v_pack - LANES
    group = LANES // rest
    spans = spans_of(k_pack, c_local)
    chunks = len(spans)
    lanes_of = [
        (first * c_local, -(-count * c_local // LANES) * LANES) for first, count in spans
    ]
    slabs = moved.shape[1]
    if k_local == k_pack:
        slabs_of = [
            (first // group * (group + 1), -(-count // group) * (group + 1)) for first, count in spans
        ]
    else:
        slabs_of = [(0, slabs)] + [None] * (chunks - 1)

    barrier = pltpu.get_barrier_semaphore()
    for step in range(1, n_fold):
        pl.semaphore_signal(barrier, device_id={"fold": (fold + step) % n_fold})
    for step in range(1, n_pair):
        pl.semaphore_signal(barrier, device_id={"pair": (pair + step) % n_pair})
    pl.semaphore_wait(barrier, n_fold + n_pair - 2)

    def to_pair(step, chunk):
        other = (pair + step) % n_pair
        first, count = slabs_of[chunk]
        return pltpu.make_async_remote_copy(
            src_ref=parts_ref.at[other, pl.ds(first, count)],
            dst_ref=moved.at[pair, pl.ds(first, count)],
            send_sem=a_send.at[other, chunk], recv_sem=a_recv.at[pair, chunk],
            device_id={"pair": other},
        )

    def from_pair(step, chunk):
        other = (pair + step) % n_pair
        first, count = slabs_of[chunk]
        return pltpu.make_async_remote_copy(
            src_ref=parts_ref.at[other, pl.ds(first, count)],
            dst_ref=moved.at[other, pl.ds(first, count)],
            send_sem=a_send.at[other, chunk], recv_sem=a_recv.at[other, chunk],
            device_id={"pair": other},
        )

    def piece_of(ref, index, chunk):
        return ref.at[(*index, slice(None), pl.ds(*lanes_of[chunk]))]

    def to_fold(target, chunk):
        return pltpu.make_async_remote_copy(
            src_ref=piece_of(wide, (target,), chunk), dst_ref=piece_of(held, (fold, pair), chunk),
            send_sem=f_send.at[target, chunk], recv_sem=f_recv.at[fold, chunk],
            device_id={"fold": target},
        )

    def from_fold(source, chunk):
        return pltpu.make_async_remote_copy(
            src_ref=piece_of(wide, (source,), chunk), dst_ref=piece_of(held, (source, pair), chunk),
            send_sem=f_send.at[source, chunk], recv_sem=f_recv.at[source, chunk],
            device_id={"fold": source},
        )

    def shared(source, other, whose, sends, recvs, mark, chunk, target):
        slot = piece_of(held, (source, whose), chunk)
        return pltpu.make_async_remote_copy(
            src_ref=slot, dst_ref=slot,
            send_sem=sends.at[source, other, chunk], recv_sem=recvs.at[source, mark, chunk],
            device_id={"pair": target},
        )

    def over_y(source, step, chunk):
        other = (y + step) % n_y
        return shared(source, other, pair, y_send, y_recv, y, chunk, other * 2 + core)

    def from_y(source, step, chunk):
        other = (y + step) % n_y
        target = other * 2 + core
        return shared(source, other, target, y_send, y_recv, other, chunk, target)

    def over_core(source, step, chunk):
        other = (y + step) % n_y
        return shared(source, other, other * 2 + core, c_send, c_recv, other, chunk, mate)

    def from_core(source, step, chunk):
        other = (y + step) % n_y
        return shared(source, other, other * 2 + 1 - core, c_send, c_recv, other, chunk, mate)

    def over_x(block):
        return pltpu.make_async_remote_copy(
            src_ref=x_out.at[block], dst_ref=x_in.at[block],
            send_sem=x_send.at[block], recv_sem=x_recv.at[block],
            device_id={"fold": outer * 2 + 1 - half},
        )

    def over_z(block, slot):
        return pltpu.make_async_remote_copy(
            src_ref=z_out.at[block], dst_ref=z_in.at[slot],
            send_sem=z_send.at[block], recv_sem=z_recv.at[slot],
            device_id={"fold": block * 2 + half},
        )

    def own_parts():
        return pltpu.make_async_copy(parts_ref.at[pair], moved.at[pair], copy_sem)

    loads = raw_w.shape[2]
    n_loads = occ_total // loads

    def load_w(step):
        slot = step % 2
        return pltpu.make_async_copy(
            w_hbm.at[:, pl.ds(step * loads, loads)], raw_w.at[slot], w_sem.at[slot]
        )

    def pack_w(step, carry):
        load_w(step).wait()
        slot = step % 2
        for k in range(loads):
            lanes = narrow(line_ref[...] ^ label_ref[step * loads + k])
            values = raw_w[slot, :, k].reshape(c_local * j_local, vir_total)
            chosen = fold_columns(values, cj_ref[...], lanes).astype(jnp.float32)
            main_w[...] = chosen[:, :LANES]
            rest_w[:, :rest] = chosen[:, LANES:]
            block = step * (loads // 4) + k // 4
            place = slice(k % 4 * c_local, (k % 4 + 1) * c_local)
            for j in range(j_local):
                own = pl.ds(j, c_local, stride=j_local)
                packed_w[j, block, place, :LANES] = main_w[own, :].astype(packed_w.dtype)
                packed_w[j, block, place, LANES:] = rest_w[own, :][:, :rest].astype(packed_w.dtype)

        @pl.when(step + 2 < n_loads)
        def _():
            load_w(step + 2).start()

        return carry

    def source_of(step):
        return flip(outer, step // 2, n_outer) * 2 + (half + 1 + step) % 2

    def relay(source, chunk):
        for step in range(1, n_y):
            over_y(source, step, chunk).start()
        over_core(source, 0, chunk).start()

    def fetch(step, chunk):
        source = source_of(step)

        @pl.when(step != 1)
        def _():
            from_fold(source, chunk).wait_recv()
            relay(source, chunk)

    def pass_on(step, chunk):
        source = source_of(step)
        for other in range(1, n_y):
            from_y(source, other, chunk).wait_recv()
            over_core(source, other, chunk).start()

    def pack_k(chunk):
        first, count = spans[chunk]
        start, width = lanes_of[chunk]
        if slabs_of[chunk] is not None:
            for step in range(1, n_pair):
                from_pair(step, chunk).wait_recv()

        def quarter(step, carry):
            q = flip(fold // here, step, FOLDS)
            labels = narrow(own_ref[...] ^ vir_ref[q])
            pieces = [[] for _ in range(here)]
            for kappa in range(first, first + count):
                chosen = jnp.zeros((rows, v_pack), moved.dtype)
                for s in range(FOLDS):
                    k = s * k_pack + kappa
                    side, inner = k // k_local, k % k_local
                    base, tail = inner // group * (group + 1), inner % group * rest
                    piece = jnp.concatenate(
                        [moved[side, base + inner % group], moved[side, base + group][:, tail:tail + rest]],
                        axis=1,
                    )
                    chosen = jnp.where(labels == occ_ref[k], piece, chosen)
                for f in range(here):
                    pieces[f].append(chosen[:, f * c_local:(f + 1) * c_local])
            spare = width - count * c_local
            for f in range(here):
                if spare:
                    pieces[f].append(jnp.zeros((rows, spare), moved.dtype))
                wide[q * here + f, :, start:start + width] = jnp.concatenate(pieces[f], axis=1)
            for f in range(here):

                @pl.when(step * here + f > 0)
                def _():
                    to_fold(q * here + (fold + f) % here, chunk).start()

            return carry

        lax.fori_loop(0, FOLDS, quarter, 0)
        own = pltpu.make_async_copy(
            piece_of(wide, (fold,), chunk), piece_of(held, (fold, pair), chunk), copy_sem
        )
        own.start()
        own.wait()
        relay(fold, chunk)

    def multiply(step, chunk):
        source = source_of(step)
        block = flip(outer, step // 2, n_outer)
        first, count = spans[chunk]
        start, depth = first * c_local, count * c_local
        for other in range(n_y):
            from_core(source, other, chunk).wait_recv()
        left = jnp.concatenate([held[source, p, :, start:start + depth] for p in range(n_pair)], axis=0)
        labels = row_ref[source]
        sums = [None] * j_local
        if chunk:
            sums = [total[source, j] for j in range(j_local)]
        for s in range(FOLDS):
            part = jnp.where(labels == col_ref[s, :, start:start + depth], left, jnp.zeros_like(left))
            place = (s * k_pack + first) // 4
            for j in range(j_local):
                right = packed_w[j, place:place + count // 4].reshape(depth, v_pack)
                term = jnp.dot(part, right, preferred_element_type=jnp.float32)
                sums[j] = term if sums[j] is None else sums[j] + term
        for j in range(j_local):
            total[source, j] = sums[j]
        if chunk < chunks - 1:
            return

        @pl.when(step % 2 == 0)
        def _():
            encode([total[source, j] for j in range(j_local)], x_out.at[block])
            over_x(block).start()

        @pl.when(step % 2 == 1)
        def _():
            over_x(block).wait_recv()
            near = decode(x_in[block], j_local, v_pack)
            near = [total[source, j] + near[j] for j in range(j_local)]

            @pl.when(step == 1)
            def _():
                for j in range(j_local):
                    out_ref[j] = near[j]

            @pl.when(step > 1)
            def _():
                encode(near, z_out.at[block])
                over_z(block, outer).start()

    for chunk in range(chunks):
        if slabs_of[chunk] is not None:
            for step in range(1, n_pair):
                to_pair(step, chunk).start()
    own_parts().start()
    load_w(0).start()
    load_w(1).start()
    own_parts().wait()
    lax.fori_loop(0, n_loads // 2, pack_w, 0)
    pack_k(0)
    lax.fori_loop(n_loads // 2, n_loads, pack_w, 0)
    for chunk in range(1, chunks):
        pack_k(chunk)

    for step in range(AHEAD):
        fetch(step, 0)
    pass_on(0, 0)
    for chunk in range(chunks):

        def source_step(step, carry):
            @pl.when(step + AHEAD < n_fold)
            def _():
                fetch(step + AHEAD, chunk)

            @pl.when(step + 1 < n_fold)
            def _():
                pass_on(step + 1, chunk)

            if chunk < chunks - 1:

                @pl.when(step + AHEAD >= n_fold)
                def _():
                    fetch(step + AHEAD - n_fold, chunk + 1)

                @pl.when(step + 1 >= n_fold)
                def _():
                    pass_on(step + 1 - n_fold, chunk + 1)

            multiply(step, chunk)
            return carry

        lax.fori_loop(0, n_fold, source_step, 0)

    def finish(step, carry):
        block = flip(outer, step, n_outer)
        over_z(block, block).wait_recv()
        far = decode(z_in[block], j_local, v_pack)
        for j in range(j_local):
            out_ref[j] += far[j]
        return carry

    lax.fori_loop(1, n_outer, finish, 0)

    for chunk in range(chunks):
        if slabs_of[chunk] is not None:
            for step in range(1, n_pair):
                to_pair(step, chunk).wait_send()

        def drain(source, carry):
            @pl.when(source != fold)
            def _():
                to_fold(source, chunk).wait_send()

            for step in range(1, n_y):
                over_y(source, step, chunk).wait_send()
            for step in range(n_y):
                over_core(source, step, chunk).wait_send()
            return carry

        lax.fori_loop(0, n_fold, drain, 0)

    def drain_sums(block, carry):
        over_x(block).wait_send()

        @pl.when(block != outer)
        def _():
            over_z(block, outer).wait_send()

        return carry

    lax.fori_loop(0, n_outer, drain_sums, 0)


def contract_all(
    n_pair, n_fold, parts, cycle_block, occ_labels, own_labels, vir_labels, cj_labels, row_labels, col_labels
):
    _, slabs, rows, _ = parts.shape
    c_local, occ_total, j_local, vir_total = cycle_block.shape
    v_pack = vir_total // FOLDS
    depth = col_labels.shape[-1]
    wide = -(-depth // LANES) * LANES
    n_y, n_outer = n_pair // 2, n_fold // 2
    count = n_pair * rows
    lanes = (j_local + -(-(j_local * (v_pack - LANES) + 1) // LANES)) * LANES
    chunks = len(spans_of(occ_total // FOLDS, c_local))
    loads = 8
    occ = jnp.broadcast_to(narrow(occ_labels)[:, None, None], (occ_total, 1, v_pack))
    sems = pltpu.SemaphoreType.DMA
    vmem = pl.BlockSpec(memory_space=pltpu.VMEM)
    kind = parts.dtype
    return pl.pallas_call(
        functools.partial(cycle_kernel, n_pair, n_fold),
        out_shape=jax.ShapeDtypeStruct((j_local, count, v_pack), jnp.float32),
        in_specs=[pl.BlockSpec(memory_space=pltpu.SMEM)] + [vmem] * 8 + [pl.BlockSpec(memory_space=pl.ANY)],
        out_specs=vmem,
        scratch_shapes=[
            pltpu.VMEM(parts.shape, kind),
            pltpu.VMEM((n_fold, rows, wide), kind),
            pltpu.VMEM((n_fold, n_pair, rows, wide), kind),
            pltpu.VMEM((j_local, occ_total // 4, 4 * c_local, v_pack), kind),
            pltpu.VMEM((2, c_local, loads, j_local, vir_total), kind),
            pltpu.VMEM((c_local * j_local, LANES), jnp.float32),
            pltpu.VMEM((c_local * j_local, LANES), jnp.float32),
            pltpu.VMEM((n_fold, j_local, count, v_pack), jnp.float32),
        ]
        + [pltpu.VMEM((n_outer, count, lanes), jnp.int16)] * 4
        + [
            sems, sems((2,)), sems((n_pair, chunks)), sems((n_pair, chunks)),
            sems((n_fold, chunks)), sems((n_fold, chunks)),
            sems((n_fold, n_y, chunks)), sems((n_fold, n_y, chunks)),
            sems((n_fold, n_y, chunks)), sems((n_fold, n_y, chunks)),
            sems((n_outer,)), sems((n_outer,)), sems((n_outer,)), sems((n_outer,)),
        ],
        compiler_params=pltpu.CompilerParams(
            collective_id=0, has_side_effects=True, vmem_limit_bytes=56 << 20
        ),
    )(
        occ_labels, occ, own_labels[:, None], vir_labels.reshape(FOLDS, 1, v_pack), vir_labels[None, :],
        narrow(cj_labels).reshape(-1, 1), narrow(row_labels), narrow(col_labels), parts, cycle_block,
    )


def body(n_pair, n_fold, amplitudes, cycle_block, occ_sizes, vir_sizes, window_i, window_occ):
    c_local, occ_total, j_local, vir_total = cycle_block.shape
    n_i, k_local, a_rows, _ = amplitudes.shape
    v_pack = vir_total // FOLDS
    k_pack = occ_total // FOLDS
    rows = n_i * a_rows // n_pair
    fold = lax.axis_index("fold")
    pair = lax.axis_index("pair")
    occ_labels = irrep_labels(occ_sizes, occ_total)
    vir_labels = irrep_labels(vir_sizes, vir_total)
    c_labels = lax.dynamic_slice_in_dim(vir_labels, fold * c_local, c_local)
    a_labels = lax.dynamic_slice_in_dim(vir_labels, fold * a_rows, a_rows)
    k_labels = lax.dynamic_slice_in_dim(occ_labels, pair * k_local, k_local)
    i_labels = label_lookup(window_i, occ_labels, occ_total)
    j_orbitals = lax.dynamic_slice_in_dim(window_occ, pair * j_local, j_local)
    j_labels = label_lookup(j_orbitals, occ_labels, occ_total)

    parts = pack_t(amplitudes, i_labels[:, None] ^ k_labels[None, :], a_labels, vir_labels, n_pair)
    ia_labels = (i_labels[:, None] ^ a_labels[None, :]).reshape(n_pair, rows)
    own_labels = lax.dynamic_slice_in_dim(ia_labels, pair, 1)[0]
    row_labels = (vir_labels.reshape(n_fold, 1, a_rows) ^ i_labels[None, :, None]).reshape(n_fold, -1, 1)
    col_labels = (occ_labels[:, None] ^ c_labels[None, :]).reshape(FOLDS, 1, k_pack * c_local)
    summed = contract_all(
        n_pair, n_fold, parts, cycle_block, occ_labels, own_labels, vir_labels,
        c_labels[:, None] ^ j_labels[None, :], row_labels, col_labels,
    )
    own = summed.astype(jnp.bfloat16).reshape(j_local, n_i, a_rows, v_pack).transpose(1, 2, 0, 3)
    iaj = i_labels[:, None, None] ^ a_labels[None, :, None] ^ j_labels[None, None, :]
    keep = iaj[..., None] == vir_labels
    return jnp.where(keep, jnp.concatenate([own] * FOLDS, axis=-1), 0)


def solution(mesh):
    sizes = mesh.shape["pair"], mesh.shape["fold"]
    placed = (P(None, "pair", "fold", None), P("fold", None, "pair", None), P(), P(), P(), P())

    def run(*args):
        return body(*sizes, *args)

    return jax.shard_map(
        run, mesh=mesh, in_specs=placed, out_specs=P(None, "fold", "pair", None), check_vma=False
    )
```

```python
import functools
import math

import jax
import jax.numpy as jnp
from jax import lax
from jax.experimental import pallas as pl
from jax.experimental.pallas import tpu as pltpu
from jax.sharding import PartitionSpec as P

LANES = 128
FOLDS = 4
AHEAD = 3
STEPS = 32000.0
FINE = 8.0


def bounds_of(sizes_ref):
    ends, total = [], 0
    for g in range(sizes_ref.shape[0]):
        total = total + sizes_ref[g]
        ends.append(total)
    return ends


def label_of(positions, ends):
    return functools.reduce(jnp.add, [jnp.where(positions >= end, 1, 0) for end in ends])


def split_by(positions, count):
    whole = jnp.floor((positions.astype(jnp.float32) + 0.5) * (1.0 / count)).astype(jnp.int32)
    return whole, positions - whole * count


def column(count):
    return lax.broadcasted_iota(jnp.int32, (count, 1), 0)


def line(count):
    return lax.broadcasted_iota(jnp.int32, (1, count), 1)


def narrow(labels):
    return labels.astype(jnp.float32).astype(jnp.bfloat16)


def fold_columns(values, rows, lanes):
    v_pack = values.shape[1] // FOLDS
    total = jnp.zeros((values.shape[0], v_pack), values.dtype)
    for q in range(FOLDS):
        cut = slice(q * v_pack, (q + 1) * v_pack)
        total = jnp.where(rows == lanes[:, cut], values[:, cut], total)
    return total


def flip(index, bits, count):
    total, bit = 0, 1
    while bit < count:
        total = total + (index // bit + bits // bit) % 2 * bit
        bit *= 2
    return total


def encode(parts, out_ref):
    top = functools.reduce(jnp.maximum, [jnp.max(jnp.abs(part), axis=1, keepdims=True) for part in parts])
    code = jnp.ceil(jnp.log2(jnp.maximum(top, 1e-30)) * FINE)
    factor = STEPS * jnp.exp2(code * (-1.0 / FINE))
    scaled = [jnp.round(part * factor).astype(jnp.int32) for part in parts]
    rest = [part[:, LANES:] for part in scaled]
    spare = LANES - sum(part.shape[1] for part in rest)
    rest.append(jnp.broadcast_to(code.astype(jnp.int32), (code.shape[0], spare)))
    for j, part in enumerate(scaled):
        out_ref[:, j * LANES:(j + 1) * LANES] = part[:, :LANES].astype(jnp.int16)
    out_ref[:, len(parts) * LANES:] = jnp.concatenate(rest, axis=1).astype(jnp.int16)


def decode(packed, count, width):
    values = packed.astype(jnp.int32).astype(jnp.float32)
    code = values[:, -1:]
    values = values * (jnp.exp2(code * (1.0 / FINE)) / STEPS)
    rest = width - LANES
    return [
        jnp.concatenate(
            [
                values[:, j * LANES:(j + 1) * LANES],
                values[:, count * LANES + j * rest:count * LANES + (j + 1) * rest],
            ],
            axis=1,
        )
        for j in range(count)
    ]


def spans_of(k_pack, c_local):
    step = LANES // math.gcd(LANES, c_local)
    return [(0, step), (step, k_pack - step)]


def cycle_kernel(
    n_pair, n_fold, occ_sizes, vir_sizes, window_i, window_occ, t_hbm, w_hbm, out_ref,
    occ_wide, occ_short, col_ref, cj_ref, parts, raw_t, moved, wide, held, packed_w, raw_w, main_w, rest_w,
    total, kept, x_out, x_in, z_out, z_in,
    copy_sem, t_sem, w_sem, a_send, a_recv, f_send, f_recv, y_send, y_recv, c_send, c_recv,
    x_send, x_recv, z_send, z_recv,
):
    pair, fold = lax.axis_index("pair"), lax.axis_index("fold")
    n_y, n_outer, here = n_pair // 2, n_fold // 2, n_fold // FOLDS
    y, core = pair // 2, pair % 2
    outer, half = fold // 2, fold % 2
    mate = y * 2 + 1 - core
    c_local, occ_total, j_local, vir_total = w_hbm.shape
    n_i, _, split, rows, _ = t_hbm.shape
    a_rows, v_pack = split * rows, vir_total // FOLDS
    k_pack, k_local = occ_total // FOLDS, occ_total // n_pair
    rest = v_pack - LANES
    group = LANES // rest
    spans = spans_of(k_pack, c_local)
    chunks = len(spans)
    lanes_of = [
        (first * c_local, -(-count * c_local // LANES) * LANES) for first, count in spans
    ]
    slabs = moved.shape[1]
    taken = spans if k_local == k_pack else [(0, k_local)] + [None] * (chunks - 1)
    slabs_of = [
        span and (span[0] // group * (group + 1), -(-span[1] // group) * (group + 1)) for span in taken
    ]

    occ_ends, vir_ends = bounds_of(occ_sizes), bounds_of(vir_sizes)
    i_labels = [label_of(window_i[i], occ_ends) for i in range(n_i)]
    j_labels = [label_of(window_occ[pair * j_local + j], occ_ends) for j in range(j_local)]
    vir_line = label_of(line(vir_total), vir_ends)

    def load_t(step, chunk):
        target = turn(step)
        first, count = taken[chunk]
        slot = step % 2
        return pltpu.make_async_copy(
            t_hbm.at[target // split, pl.ds(first, count), target % split],
            raw_t.at[slot, pl.ds(0, count)], t_sem.at[slot],
        )

    def turn(step):
        return (y + 1 + step // 2) % n_y * 2 + (core + 1 + step) % 2

    def to_pair(step, chunk):
        other = turn(step)
        first, count = slabs_of[chunk]
        return pltpu.make_async_remote_copy(
            src_ref=parts.at[other, pl.ds(first, count)],
            dst_ref=moved.at[pair, pl.ds(first, count)],
            send_sem=a_send.at[other, chunk], recv_sem=a_recv.at[pair, chunk],
            device_id={"pair": other},
        )

    def from_pair(step, chunk):
        other = turn(step)
        first, count = slabs_of[chunk]
        return pltpu.make_async_remote_copy(
            src_ref=parts.at[other, pl.ds(first, count)],
            dst_ref=moved.at[other, pl.ds(first, count)],
            send_sem=a_send.at[other, chunk], recv_sem=a_recv.at[other, chunk],
            device_id={"pair": other},
        )

    def piece_of(ref, index, chunk):
        return ref.at[(*index, slice(None), pl.ds(*lanes_of[chunk]))]

    def to_fold(target, chunk):
        return pltpu.make_async_remote_copy(
            src_ref=piece_of(wide, (target,), chunk), dst_ref=piece_of(held, (fold, pair), chunk),
            send_sem=f_send.at[target, chunk], recv_sem=f_recv.at[fold, chunk],
            device_id={"fold": target},
        )

    def from_fold(source, chunk):
        return pltpu.make_async_remote_copy(
            src_ref=piece_of(wide, (source,), chunk), dst_ref=piece_of(held, (source, pair), chunk),
            send_sem=f_send.at[source, chunk], recv_sem=f_recv.at[source, chunk],
            device_id={"fold": source},
        )

    def shared(source, other, whose, sends, recvs, mark, chunk, target):
        slot = piece_of(held, (source, whose), chunk)
        return pltpu.make_async_remote_copy(
            src_ref=slot, dst_ref=slot,
            send_sem=sends.at[source, other, chunk], recv_sem=recvs.at[source, mark, chunk],
            device_id={"pair": target},
        )

    def over_y(source, step, chunk):
        other = (y + step) % n_y
        return shared(source, other, pair, y_send, y_recv, y, chunk, other * 2 + core)

    def from_y(source, step, chunk):
        other = (y + step) % n_y
        target = other * 2 + core
        return shared(source, other, target, y_send, y_recv, other, chunk, target)

    def over_core(source, step, chunk):
        other = (y + step) % n_y
        return shared(source, other, other * 2 + core, c_send, c_recv, other, chunk, mate)

    def from_core(source, step, chunk):
        other = (y + step) % n_y
        return shared(source, other, other * 2 + 1 - core, c_send, c_recv, other, chunk, mate)

    def over_x(block):
        return pltpu.make_async_remote_copy(
            src_ref=x_out.at[block], dst_ref=x_in.at[block],
            send_sem=x_send.at[block], recv_sem=x_recv.at[block],
            device_id={"fold": outer * 2 + 1 - half},
        )

    def over_z(block, slot):
        return pltpu.make_async_remote_copy(
            src_ref=z_out.at[block], dst_ref=z_in.at[slot],
            send_sem=z_send.at[block], recv_sem=z_recv.at[slot],
            device_id={"fold": block * 2 + half},
        )

    def own_parts(chunk):
        first, count = slabs_of[chunk]
        return pltpu.make_async_copy(
            parts.at[pair, pl.ds(first, count)], moved.at[pair, pl.ds(first, count)], copy_sem
        )

    def pack_t(chunk):
        first, count = taken[chunk]

        def one(step, carry):
            target = turn(step)
            load_t(step, chunk).wait()
            slot = step % 2
            own_rows = narrow(
                label_of(fold * a_rows + target % split * rows + column(rows), vir_ends)
            )
            i_label = label_of(window_i[target // split], occ_ends)
            tails = []
            for k in range(first, first + count):
                lanes = narrow(vir_line ^ occ_wide[pair * k_local + k] ^ i_label)
                chosen = fold_columns(raw_t[slot, k - first], own_rows, lanes)
                base = k // group * (group + 1)
                parts[target, base + k % group] = chosen[:, :LANES]
                tails.append(chosen[:, LANES:])
                if k == k_local - 1:
                    tails += [jnp.zeros_like(tails[0])] * (group - len(tails))
                if len(tails) == group:
                    parts[target, base + group] = jnp.concatenate(tails, axis=1)
                    tails = []

            @pl.when(step < n_pair - 1)
            def _():
                to_pair(step, chunk).start()

            @pl.when(step + 2 < n_pair)
            def _():
                load_t(step + 2, chunk).start()

            if chunk + 1 < chunks and taken[chunk + 1] is not None:

                @pl.when(step + 2 >= n_pair)
                def _():
                    load_t(step + 2 - n_pair, chunk + 1).start()

            return carry

        lax.fori_loop(0, n_pair, one, 0)
        own_parts(chunk).start()
        own_parts(chunk).wait()

    loads = raw_w.shape[2]
    n_loads = occ_total // loads

    def load_w(step):
        slot = step % 2
        return pltpu.make_async_copy(
            w_hbm.at[:, pl.ds(step * loads, loads)], raw_w.at[slot], w_sem.at[slot]
        )

    def pack_w(step, carry):
        load_w(step).wait()
        slot = step % 2
        for k in range(loads):
            lanes = narrow(vir_line ^ occ_wide[step * loads + k])
            values = raw_w[slot, :, k].reshape(c_local * j_local, vir_total)
            chosen = fold_columns(values, narrow(cj_ref[...]), lanes).astype(jnp.float32)
            main_w[...] = chosen[:, :LANES]
            rest_w[:, :rest] = chosen[:, LANES:]
            block = step * (loads // 4) + k // 4
            place = slice(k % 4 * c_local, (k % 4 + 1) * c_local)
            for j in range(j_local):
                own = pl.ds(j, c_local, stride=j_local)
                packed_w[j, block, place, :LANES] = main_w[own, :].astype(packed_w.dtype)
                packed_w[j, block, place, LANES:] = rest_w[own, :][:, :rest].astype(packed_w.dtype)

        @pl.when(step + 2 < n_loads)
        def _():
            load_w(step + 2).start()

        return carry

    def source_of(step):
        return flip(outer, step // 2, n_outer) * 2 + (half + 1 + step) % 2

    def relay(source, chunk):
        for step in range(1, n_y):
            over_y(source, step, chunk).start()
        over_core(source, 0, chunk).start()

    def fetch(step, chunk):
        source = source_of(step)

        @pl.when(step != 1)
        def _():
            from_fold(source, chunk).wait_recv()
            relay(source, chunk)

    def pass_on(step, chunk):
        source = source_of(step)
        for other in range(1, n_y):
            from_y(source, other, chunk).wait_recv()
            over_core(source, other, chunk).start()

    def pack_k(chunk):
        first, count = spans[chunk]
        start, width = lanes_of[chunk]
        if slabs_of[chunk] is not None:
            for step in range(n_pair - 1):
                from_pair(step, chunk).wait_recv()
        own_rows = label_of(fold * a_rows + pair % split * rows + column(rows), vir_ends)
        own_rows = own_rows ^ label_of(window_i[pair // split], occ_ends)

        def quarter(step, carry):
            q = flip(fold // here, step, FOLDS)
            labels = narrow(own_rows ^ label_of(q * v_pack + line(v_pack), vir_ends))
            pieces = [[] for _ in range(here)]
            for kappa in range(first, first + count):
                chosen = jnp.zeros((rows, v_pack), moved.dtype)
                for s in range(FOLDS):
                    k = s * k_pack + kappa
                    side, inner = k // k_local, k % k_local
                    base, tail = inner // group * (group + 1), inner % group * rest
                    piece = jnp.concatenate(
                        [moved[side, base + inner % group], moved[side, base + group][:, tail:tail + rest]],
                        axis=1,
                    )
                    chosen = jnp.where(labels == occ_short[k], piece, chosen)
                for f in range(here):
                    pieces[f].append(chosen[:, f * c_local:(f + 1) * c_local])
            spare = width - count * c_local
            for f in range(here):
                if spare:
                    pieces[f].append(jnp.zeros((rows, spare), moved.dtype))
                wide[q * here + f, :, start:start + width] = jnp.concatenate(pieces[f], axis=1)
            for f in range(here):

                @pl.when(step * here + f > 0)
                def _():
                    to_fold(q * here + (fold + f) % here, chunk).start()

            return carry

        lax.fori_loop(0, FOLDS, quarter, 0)
        own = pltpu.make_async_copy(
            piece_of(wide, (fold,), chunk), piece_of(held, (fold, pair), chunk), copy_sem
        )
        own.start()
        own.wait()
        relay(fold, chunk)

    def multiply(step, chunk):
        source = source_of(step)
        block = flip(outer, step // 2, n_outer)
        first, count = spans[chunk]
        start, depth = first * c_local, count * c_local
        for other in range(n_y):
            from_core(source, other, chunk).wait_recv()
        left = jnp.concatenate([held[source, p, :, start:start + depth] for p in range(n_pair)], axis=0)
        own_rows = label_of(source * a_rows + column(a_rows), vir_ends)
        labels = narrow(jnp.concatenate([own_rows ^ i_label for i_label in i_labels], axis=0))
        sums = [None] * j_local
        if chunk:
            sums = [total[source, j] for j in range(j_local)]
        for s in range(FOLDS):
            part = jnp.where(labels == col_ref[s, :, start:start + depth], left, jnp.zeros_like(left))
            place = (s * k_pack + first) // 4
            for j in range(j_local):
                right = packed_w[j, place:place + count // 4].reshape(depth, v_pack)
                term = jnp.dot(part, right, preferred_element_type=jnp.float32)
                sums[j] = term if sums[j] is None else sums[j] + term
        for j in range(j_local):
            total[source, j] = sums[j]
        if chunk < chunks - 1:
            return

        @pl.when(step % 2 == 0)
        def _():
            encode([total[source, j] for j in range(j_local)], x_out.at[block])
            over_x(block).start()

        @pl.when(step % 2 == 1)
        def _():
            over_x(block).wait_recv()
            near = decode(x_in[block], j_local, v_pack)
            near = [total[source, j] + near[j] for j in range(j_local)]

            @pl.when(step == 1)
            def _():
                for j in range(j_local):
                    kept[j] = near[j]

            @pl.when(step > 1)
            def _():
                encode(near, z_out.at[block])
                over_z(block, outer).start()

    load_t(0, 0).start()
    load_t(1, 0).start()
    load_w(0).start()
    load_w(1).start()
    places = lax.broadcasted_iota(jnp.int32, (occ_total, 1, vir_total), 0)
    occ_wide[...] = label_of(places, occ_ends)
    occ_short[...] = narrow(label_of(places[:, :, :v_pack], occ_ends))
    c_of, j_of = split_by(column(c_local * j_local), j_local)
    j_mixed = functools.reduce(jnp.add, [jnp.where(j_of == j, j_labels[j], 0) for j in range(j_local)])
    cj_ref[...] = label_of(fold * c_local + c_of, vir_ends) ^ j_mixed
    kappa_of, c_of = split_by(line(k_pack * c_local), c_local)
    c_mixed = label_of(fold * c_local + c_of, vir_ends)
    for s in range(FOLDS):
        col_ref[s] = narrow(label_of(s * k_pack + kappa_of, occ_ends) ^ c_mixed)
    barrier = pltpu.get_barrier_semaphore()
    for step in range(1, n_fold):
        pl.semaphore_signal(barrier, device_id={"fold": (fold + step) % n_fold})
    for step in range(1, n_pair):
        pl.semaphore_signal(barrier, device_id={"pair": (pair + step) % n_pair})
    pl.semaphore_wait(barrier, n_fold + n_pair - 2)

    for chunk in range(chunks):
        if taken[chunk] is not None:
            pack_t(chunk)
    lax.fori_loop(0, n_loads // 2, pack_w, 0)
    pack_k(0)
    lax.fori_loop(n_loads // 2, n_loads, pack_w, 0)
    for chunk in range(1, chunks):
        pack_k(chunk)

    for step in range(AHEAD):
        fetch(step, 0)
    pass_on(0, 0)
    for chunk in range(chunks):

        def source_step(step, carry):
            @pl.when(step + AHEAD < n_fold)
            def _():
                fetch(step + AHEAD, chunk)

            @pl.when(step + 1 < n_fold)
            def _():
                pass_on(step + 1, chunk)

            if chunk < chunks - 1:

                @pl.when(step + AHEAD >= n_fold)
                def _():
                    fetch(step + AHEAD - n_fold, chunk + 1)

                @pl.when(step + 1 >= n_fold)
                def _():
                    pass_on(step + 1 - n_fold, chunk + 1)

            multiply(step, chunk)
            return carry

        lax.fori_loop(0, n_fold, source_step, 0)

    def finish(step, carry):
        block = flip(outer, step, n_outer)
        over_z(block, block).wait_recv()
        far = decode(z_in[block], j_local, v_pack)
        for j in range(j_local):
            kept[j] += far[j]
        return carry

    lax.fori_loop(1, n_outer, finish, 0)

    for i in range(n_i):
        for j in range(j_local):
            own = pl.ds(j, a_rows, stride=j_local)
            values = kept[j, i * a_rows:(i + 1) * a_rows]
            main_w[own, :] = values[:, :LANES]
            rest_w[own, :rest] = values[:, LANES:]
        values = jnp.concatenate([main_w[...], rest_w[:, :rest]], axis=1)
        labels = cj_ref[...] ^ i_labels[i]
        full = [
            jnp.where(labels == vir_line[:, q * v_pack:(q + 1) * v_pack], values, 0.0) for q in range(FOLDS)
        ]
        full = jnp.concatenate(full, axis=1).astype(out_ref.dtype)
        out_ref[i] = full.reshape(a_rows, j_local, vir_total)

    for chunk in range(chunks):
        if slabs_of[chunk] is not None:
            for step in range(n_pair - 1):
                to_pair(step, chunk).wait_send()

        def drain(source, carry):
            @pl.when(source != fold)
            def _():
                to_fold(source, chunk).wait_send()

            for step in range(1, n_y):
                over_y(source, step, chunk).wait_send()
            for step in range(n_y):
                over_core(source, step, chunk).wait_send()
            return carry

        lax.fori_loop(0, n_fold, drain, 0)

    def drain_sums(block, carry):
        over_x(block).wait_send()

        @pl.when(block != outer)
        def _():
            over_z(block, outer).wait_send()

        return carry

    lax.fori_loop(0, n_outer, drain_sums, 0)


def body(n_pair, n_fold, amplitudes, cycle_block, occ_sizes, vir_sizes, window_i, window_occ):
    c_local, occ_total, j_local, vir_total = cycle_block.shape
    n_i, k_local, a_rows, _ = amplitudes.shape
    v_pack = vir_total // FOLDS
    split = n_pair // n_i
    rows = a_rows // split
    group = LANES // (v_pack - LANES)
    slabs = -(-k_local // group) * (group + 1)
    depth = occ_total // FOLDS * c_local
    wide = -(-depth // LANES) * LANES
    n_y, n_outer = n_pair // 2, n_fold // 2
    count = n_pair * rows
    lanes = (j_local + -(-(j_local * (v_pack - LANES) + 1) // LANES)) * LANES
    spans = spans_of(occ_total // FOLDS, c_local)
    chunks = len(spans)
    most = max(span[1] for span in spans) if k_local * FOLDS == occ_total else k_local
    loads = 8
    sems = pltpu.SemaphoreType.DMA
    smem = pl.BlockSpec(memory_space=pltpu.SMEM)
    hbm = pl.BlockSpec(memory_space=pl.ANY)
    kind = amplitudes.dtype
    return pl.pallas_call(
        functools.partial(cycle_kernel, n_pair, n_fold),
        out_shape=jax.ShapeDtypeStruct((n_i, a_rows, j_local, vir_total), kind),
        in_specs=[smem] * 4 + [hbm] * 2,
        out_specs=pl.BlockSpec(memory_space=pltpu.VMEM),
        scratch_shapes=[
            pltpu.VMEM((occ_total, 1, vir_total), jnp.int32),
            pltpu.VMEM((occ_total, 1, v_pack), kind),
            pltpu.VMEM((FOLDS, 1, depth), kind),
            pltpu.VMEM((c_local * j_local, 1), jnp.int32),
            pltpu.VMEM((n_pair, slabs, rows, LANES), kind),
            pltpu.VMEM((2, most, rows, vir_total), kind),
            pltpu.VMEM((n_pair, slabs, rows, LANES), kind),
            pltpu.VMEM((n_fold, rows, wide), kind),
            pltpu.VMEM((n_fold, n_pair, rows, wide), kind),
            pltpu.VMEM((j_local, occ_total // 4, 4 * c_local, v_pack), kind),
            pltpu.VMEM((2, c_local, loads, j_local, vir_total), kind),
            pltpu.VMEM((c_local * j_local, LANES), jnp.float32),
            pltpu.VMEM((c_local * j_local, LANES), jnp.float32),
            pltpu.VMEM((n_fold, j_local, count, v_pack), jnp.float32),
            pltpu.VMEM((j_local, count, v_pack), jnp.float32),
        ]
        + [pltpu.VMEM((n_outer, count, lanes), jnp.int16)] * 4
        + [
            sems, sems((2,)), sems((2,)), sems((n_pair, chunks)), sems((n_pair, chunks)),
            sems((n_fold, chunks)), sems((n_fold, chunks)),
            sems((n_fold, n_y, chunks)), sems((n_fold, n_y, chunks)),
            sems((n_fold, n_y, chunks)), sems((n_fold, n_y, chunks)),
            sems((n_outer,)), sems((n_outer,)), sems((n_outer,)), sems((n_outer,)),
        ],
        compiler_params=pltpu.CompilerParams(
            collective_id=0, has_side_effects=True, vmem_limit_bytes=60 << 20
        ),
    )(
        occ_sizes, vir_sizes, window_i, window_occ,
        amplitudes.reshape(n_i, k_local, split, rows, vir_total), cycle_block,
    )


def solution(mesh):
    sizes = mesh.shape["pair"], mesh.shape["fold"]
    placed = (P(None, "pair", "fold", None), P("fold", None, "pair", None), P(), P(), P(), P())

    def run(*args):
        return body(*sizes, *args)

    return jax.shard_map(
        run, mesh=mesh, in_specs=placed, out_specs=P(None, "fold", "pair", None), check_vma=False
    )
```

```python
import functools
import math

import jax
import jax.numpy as jnp
from jax import lax
from jax.experimental import pallas as pl
from jax.experimental.pallas import tpu as pltpu
from jax.sharding import PartitionSpec as P

LANES = 128
FOLDS = 4
EARLY = 2
READY = 6
AHEAD = 3
NEXT = 1
STEPS = 32000.0
FINE = 8.0


def bounds_of(sizes_ref):
    ends, total = [], 0
    for g in range(sizes_ref.shape[0]):
        total = total + sizes_ref[g]
        ends.append(total)
    return ends


def label_of(positions, ends):
    return functools.reduce(jnp.add, [jnp.where(positions >= end, 1, 0) for end in ends])


def split_by(positions, count):
    whole = jnp.floor((positions.astype(jnp.float32) + 0.5) * (1.0 / count)).astype(jnp.int32)
    return whole, positions - whole * count


def column(count):
    return lax.broadcasted_iota(jnp.int32, (count, 1), 0)


def line(count):
    return lax.broadcasted_iota(jnp.int32, (1, count), 1)


def narrow(labels):
    return labels.astype(jnp.float32).astype(jnp.bfloat16)


def fold_columns(values, rows, lanes):
    v_pack = values.shape[1] // FOLDS
    total = jnp.zeros((values.shape[0], v_pack), values.dtype)
    for q in range(FOLDS):
        cut = slice(q * v_pack, (q + 1) * v_pack)
        total = jnp.where(rows == lanes[:, cut], values[:, cut], total)
    return total


def flip(index, bits, count):
    total, bit = 0, 1
    while bit < count:
        total = total + (index // bit + bits // bit) % 2 * bit
        bit *= 2
    return total


def encode(parts, out_ref):
    top = functools.reduce(jnp.maximum, [jnp.max(jnp.abs(part), axis=1, keepdims=True) for part in parts])
    code = jnp.ceil(jnp.log2(jnp.maximum(top, 1e-30)) * FINE)
    factor = STEPS * jnp.exp2(code * (-1.0 / FINE))
    scaled = [jnp.round(part * factor).astype(jnp.int32) for part in parts]
    rest = [part[:, LANES:] for part in scaled]
    spare = LANES - sum(part.shape[1] for part in rest)
    rest.append(jnp.broadcast_to(code.astype(jnp.int32), (code.shape[0], spare)))
    for j, part in enumerate(scaled):
        out_ref[:, j * LANES:(j + 1) * LANES] = part[:, :LANES].astype(jnp.int16)
    out_ref[:, len(parts) * LANES:] = jnp.concatenate(rest, axis=1).astype(jnp.int16)


def decode(packed, count, width):
    values = packed.astype(jnp.int32).astype(jnp.float32)
    code = values[:, -1:]
    values = values * (jnp.exp2(code * (1.0 / FINE)) / STEPS)
    rest = width - LANES
    return [
        jnp.concatenate(
            [
                values[:, j * LANES:(j + 1) * LANES],
                values[:, count * LANES + j * rest:count * LANES + (j + 1) * rest],
            ],
            axis=1,
        )
        for j in range(count)
    ]


def spans_of(k_pack, c_local):
    step = LANES // math.gcd(LANES, c_local)
    return [(0, step), (step, k_pack - step)]


def cycle_kernel(
    n_pair, n_fold, occ_sizes, vir_sizes, window_i, window_occ, t_hbm, w_hbm, out_ref,
    occ_wide, col_ref, cj_ref, parts, raw_t, moved, wide, held, packed_w, raw_w, main_w, rest_w,
    total, kept, x_out, x_in, z_out, z_in, m_in,
    copy_sem, t_sem, w_sem, a_send, a_recv, f_send, f_recv, y_send, y_recv, c_send, c_recv,
    x_send, x_recv, z_send, z_recv, m_recv,
):
    pair, fold = lax.axis_index("pair"), lax.axis_index("fold")
    n_y, n_outer, here = n_pair // 2, n_fold // 2, n_fold // FOLDS
    y, core = pair // 2, pair % 2
    outer, half = fold // 2, fold % 2
    mate = y * 2 + 1 - core
    c_local, occ_total, j_local, vir_total = w_hbm.shape
    n_i, _, split, rows, _ = t_hbm.shape
    a_rows, v_pack = split * rows, vir_total // FOLDS
    k_pack, k_local = occ_total // FOLDS, occ_total // n_pair
    rest = v_pack - LANES
    group = LANES // rest
    spans = spans_of(k_pack, c_local)
    chunks = len(spans)
    lanes_of = [
        (first * c_local, -(-count * c_local // LANES) * LANES) for first, count in spans
    ]
    slabs = moved.shape[1]
    taken = spans if k_local == k_pack else [(0, k_local)] + [None] * (chunks - 1)
    slabs_of = [
        span and (span[0] // group * (group + 1), -(-span[1] // group) * (group + 1)) for span in taken
    ]

    occ_ends, vir_ends = bounds_of(occ_sizes), bounds_of(vir_sizes)
    i_labels = [label_of(window_i[i], occ_ends) for i in range(n_i)]
    j_labels = [label_of(window_occ[pair * j_local + j], occ_ends) for j in range(j_local)]
    vir_line = label_of(line(vir_total), vir_ends)

    def load_t(step, chunk):
        target = turn(step)
        first, count = taken[chunk]
        slot = step % 2
        return pltpu.make_async_copy(
            t_hbm.at[target // split, pl.ds(first, count), target % split],
            raw_t.at[slot, pl.ds(0, count)], t_sem.at[slot],
        )

    def turn(step):
        return (y + 1 + step // 2) % n_y * 2 + (core + 1 + step) % 2

    def to_pair(step, chunk):
        other = turn(step)
        first, count = slabs_of[chunk]
        return pltpu.make_async_remote_copy(
            src_ref=parts.at[other, pl.ds(first, count)],
            dst_ref=moved.at[pair, pl.ds(first, count)],
            send_sem=a_send.at[other, chunk], recv_sem=a_recv.at[pair, chunk],
            device_id={"pair": other},
        )

    def from_pair(step, chunk):
        other = turn(step)
        first, count = slabs_of[chunk]
        return pltpu.make_async_remote_copy(
            src_ref=parts.at[other, pl.ds(first, count)],
            dst_ref=moved.at[other, pl.ds(first, count)],
            send_sem=a_send.at[other, chunk], recv_sem=a_recv.at[other, chunk],
            device_id={"pair": other},
        )

    def piece_of(ref, index, chunk):
        return ref.at[(*index, slice(None), pl.ds(*lanes_of[chunk]))]

    def to_fold(target, chunk):
        return pltpu.make_async_remote_copy(
            src_ref=piece_of(wide, (target,), chunk), dst_ref=piece_of(held, (fold, pair), chunk),
            send_sem=f_send.at[target, chunk], recv_sem=f_recv.at[fold, chunk],
            device_id={"fold": target},
        )

    def from_fold(source, chunk):
        return pltpu.make_async_remote_copy(
            src_ref=piece_of(wide, (source,), chunk), dst_ref=piece_of(held, (source, pair), chunk),
            send_sem=f_send.at[source, chunk], recv_sem=f_recv.at[source, chunk],
            device_id={"fold": source},
        )

    def shared(source, other, whose, sends, recvs, mark, chunk, target):
        slot = piece_of(held, (source, whose), chunk)
        return pltpu.make_async_remote_copy(
            src_ref=slot, dst_ref=slot,
            send_sem=sends.at[source, other, chunk], recv_sem=recvs.at[source, mark, chunk],
            device_id={"pair": target},
        )

    def over_y(source, step, chunk):
        other = (y + step) % n_y
        return shared(source, other, pair, y_send, y_recv, y, chunk, other * 2 + core)

    def from_y(source, step, chunk):
        other = (y + step) % n_y
        target = other * 2 + core
        return shared(source, other, target, y_send, y_recv, other, chunk, target)

    def over_core(source, step, chunk):
        other = (y + step) % n_y
        return shared(source, other, other * 2 + core, c_send, c_recv, other, chunk, mate)

    def from_core(source, step, chunk):
        other = (y + step) % n_y
        return shared(source, other, other * 2 + 1 - core, c_send, c_recv, other, chunk, mate)

    def over_x(block):
        return pltpu.make_async_remote_copy(
            src_ref=x_out.at[block], dst_ref=x_in.at[block],
            send_sem=x_send.at[block], recv_sem=x_recv.at[block],
            device_id={"fold": outer * 2 + 1 - half},
        )

    def over_z(block, slot):
        return pltpu.make_async_remote_copy(
            src_ref=z_out.at[block], dst_ref=z_in.at[slot],
            send_sem=z_send.at[block], recv_sem=z_recv.at[slot],
            device_id={"fold": block * 2 + half},
        )

    def to_near(block):
        return pltpu.make_async_remote_copy(
            src_ref=z_out.at[block], dst_ref=m_in.at[block],
            send_sem=z_send.at[block], recv_sem=m_recv.at[block],
            device_id={"fold": flip(outer, 1, n_outer) * 2 + half},
        )

    def own_parts(chunk):
        first, count = slabs_of[chunk]
        return pltpu.make_async_copy(
            parts.at[pair, pl.ds(first, count)], moved.at[pair, pl.ds(first, count)], copy_sem
        )

    def pack_t(chunk):
        first, count = taken[chunk]

        def one(step, carry):
            target = turn(step)
            load_t(step, chunk).wait()
            slot = step % 2
            own_rows = narrow(
                label_of(fold * a_rows + target % split * rows + column(rows), vir_ends)
            )
            i_label = label_of(window_i[target // split], occ_ends)
            tails = []
            for k in range(first, first + count):
                lanes = narrow(vir_line ^ occ_wide[pl.ds(pair * k_local + k, 1), :] ^ i_label)
                chosen = fold_columns(raw_t[slot, k - first], own_rows, lanes)
                base = k // group * (group + 1)
                parts[target, base + k % group] = chosen[:, :LANES]
                tails.append(chosen[:, LANES:])
                if k == k_local - 1:
                    tails += [jnp.zeros_like(tails[0])] * (group - len(tails))
                if len(tails) == group:
                    parts[target, base + group] = jnp.concatenate(tails, axis=1)
                    tails = []

            @pl.when(step < n_pair - 1)
            def _():
                to_pair(step, chunk).start()

            @pl.when(step + 2 < n_pair)
            def _():
                load_t(step + 2, chunk).start()

            if chunk + 1 < chunks and taken[chunk + 1] is not None:

                @pl.when(step + 2 >= n_pair)
                def _():
                    load_t(step + 2 - n_pair, chunk + 1).start()

            return carry

        lax.fori_loop(0, n_pair, one, 0)
        own_parts(chunk).start()
        own_parts(chunk).wait()

    loads = raw_w.shape[2]
    n_loads = occ_total // loads

    def load_w(step):
        slot = step % 2
        return pltpu.make_async_copy(
            w_hbm.at[:, pl.ds(step * loads, loads)], raw_w.at[slot], w_sem.at[slot]
        )

    def pack_w(step, carry):
        load_w(step).wait()
        slot = step % 2
        for k in range(loads):
            lanes = narrow(vir_line ^ occ_wide[pl.ds(step * loads + k, 1), :])
            values = raw_w[slot, :, k].reshape(c_local * j_local, vir_total)
            chosen = fold_columns(values, narrow(cj_ref[...]), lanes).astype(jnp.float32)
            main_w[...] = chosen[:, :LANES]
            rest_w[:, :rest] = chosen[:, LANES:]
            block = step * (loads // 4) + k // 4
            place = slice(k % 4 * c_local, (k % 4 + 1) * c_local)
            for j in range(j_local):
                own = pl.ds(j, c_local, stride=j_local)
                packed_w[j, block, place, :LANES] = main_w[own, :].astype(packed_w.dtype)
                packed_w[j, block, place, LANES:] = rest_w[own, :][:, :rest].astype(packed_w.dtype)

        @pl.when(step + 2 < n_loads)
        def _():
            load_w(step + 2).start()

        return carry

    def block_of(step, chunk):
        return flip(outer, (step // 2 + (chunk == chunks - 1)) % n_outer, n_outer)

    def source_of(step, chunk):
        return block_of(step, chunk) * 2 + (half + 1 + step) % 2

    def relay(source, chunk):
        for step in range(1, n_y):
            over_y(source, step, chunk).start()
        over_core(source, 0, chunk).start()

    def fetch(step, chunk):
        source = source_of(step, chunk)

        @pl.when(source != fold)
        def _():
            from_fold(source, chunk).wait_recv()
            relay(source, chunk)


    def pass_on(step, chunk):
        source = source_of(step, chunk)
        for other in range(1, n_y):
            from_y(source, other, chunk).wait_recv()
            over_core(source, other, chunk).start()

    def pack_k(chunk):
        first, count = spans[chunk]
        start, width = lanes_of[chunk]
        if slabs_of[chunk] is not None:
            for step in range(n_pair - 1):
                from_pair(step, chunk).wait_recv()
        own_rows = label_of(fold * a_rows + pair % split * rows + column(rows), vir_ends)
        own_rows = own_rows ^ label_of(window_i[pair // split], occ_ends)

        def quarter(step, carry):
            q = flip(fold // here, step, FOLDS)
            labels = narrow(own_rows ^ label_of(q * v_pack + line(v_pack), vir_ends))
            pieces = [[] for _ in range(here)]
            for kappa in range(first, first + count):
                chosen = jnp.zeros((rows, v_pack), moved.dtype)
                for s in range(FOLDS):
                    k = s * k_pack + kappa
                    side, inner = k // k_local, k % k_local
                    base, tail = inner // group * (group + 1), inner % group * rest
                    piece = jnp.concatenate(
                        [moved[side, base + inner % group], moved[side, base + group][:, tail:tail + rest]],
                        axis=1,
                    )
                    chosen = jnp.where(labels == narrow(occ_wide[k:k + 1, :v_pack]), piece, chosen)
                for f in range(here):
                    pieces[f].append(chosen[:, f * c_local:(f + 1) * c_local])
            spare = width - count * c_local
            for f in range(here):
                if spare:
                    pieces[f].append(jnp.zeros((rows, spare), moved.dtype))
                wide[q * here + f, :, start:start + width] = jnp.concatenate(pieces[f], axis=1)
            for f in range(here):

                @pl.when(step * here + f > 0)
                def _():
                    to_fold(q * here + (fold + f) % here, chunk).start()

            return carry

        lax.fori_loop(0, FOLDS, quarter, 0)
        own = pltpu.make_async_copy(
            piece_of(wide, (fold,), chunk), piece_of(held, (fold, pair), chunk), copy_sem
        )
        own.start()
        own.wait()
        relay(fold, chunk)

    def multiply(step, chunk):
        source = source_of(step, chunk)
        block = block_of(step, chunk)
        first, count = spans[chunk]
        start, depth = first * c_local, count * c_local
        for other in range(n_y):
            from_core(source, other, chunk).wait_recv()
        left = jnp.concatenate([held[source, p, :, start:start + depth] for p in range(n_pair)], axis=0)
        own_rows = label_of(source * a_rows + column(a_rows), vir_ends)
        labels = narrow(jnp.concatenate([own_rows ^ i_label for i_label in i_labels], axis=0))
        sums = [None] * j_local
        if chunk:
            sums = [total[source, j] for j in range(j_local)]
        for s in range(FOLDS):
            part = jnp.where(labels == col_ref[s, :, start:start + depth], left, jnp.zeros_like(left))
            place = (s * k_pack + first) // 4
            for j in range(j_local):
                right = packed_w[j, place:place + count // 4].reshape(depth, v_pack)
                term = jnp.dot(part, right, preferred_element_type=jnp.float32)
                sums[j] = term if sums[j] is None else sums[j] + term
        for j in range(j_local):
            total[source, j] = sums[j]
        if chunk < chunks - 1:
            return

        @pl.when(step % 2 == 0)
        def _():
            encode([total[source, j] for j in range(j_local)], x_out.at[block])
            over_x(block).start()

        @pl.when((step % 2 == 1) & (step > 1))
        def _():
            settle(step // 2)

    def settle(turned):
        block = flip(outer, turned, n_outer)
        over_x(block).wait_recv()
        near = decode(x_in[block], j_local, v_pack)
        near = [total[block * 2 + half, j] + near[j] for j in range(j_local)]
        late = 0 if isinstance(turned, int) else 1
        for j in range(j_local):
            kept[late, j] = near[j]

        @pl.when((turned % 2 == 1) & (turned > 1))
        def _():
            to_near(block).wait_recv()
            more = decode(m_in[block], j_local, v_pack)
            for j in range(j_local):
                kept[1, j] += more[j]

        @pl.when(turned > 0)
        def _():
            encode([kept[1, j] for j in range(j_local)], z_out.at[block])

        @pl.when((turned % 2 == 0) & (turned > 0))
        def _():
            to_near(block).start()

        @pl.when(turned % 2 == 1)
        def _():
            over_z(block, outer).start()

    load_t(0, 0).start()
    load_t(1, 0).start()
    load_w(0).start()
    load_w(1).start()
    barrier = pltpu.get_barrier_semaphore()
    for step in range(1, n_fold):
        pl.semaphore_signal(barrier, device_id={"fold": (fold + step) % n_fold})
    for step in range(1, n_pair):
        pl.semaphore_signal(barrier, device_id={"pair": (pair + step) % n_pair})

    occ_wide[...] = label_of(lax.broadcasted_iota(jnp.int32, (occ_total, vir_total), 0), occ_ends)
    pl.semaphore_wait(barrier, n_fold + n_pair - 2)
    for chunk in range(chunks):
        if taken[chunk] is not None:
            pack_t(chunk)
    c_of, j_of = split_by(column(c_local * j_local), j_local)
    j_mixed = functools.reduce(jnp.add, [jnp.where(j_of == j, j_labels[j], 0) for j in range(j_local)])
    cj_ref[...] = label_of(fold * c_local + c_of, vir_ends) ^ j_mixed
    kappa_of, c_of = split_by(line(k_pack * c_local), c_local)
    c_mixed = label_of(fold * c_local + c_of, vir_ends)
    for s in range(FOLDS):
        col_ref[s] = narrow(label_of(s * k_pack + kappa_of, occ_ends) ^ c_mixed)
    lax.fori_loop(0, EARLY, pack_w, 0)
    pack_k(0)

    def pack_w_relaying(step, carry):
        pack_w(step, carry)

        @pl.when((step > EARLY) & (step <= EARLY + READY))
        def _():
            fetch(step - EARLY - 1, 0)

        return carry

    lax.fori_loop(EARLY, n_loads, pack_w_relaying, 0)
    for chunk in range(1, chunks):
        pack_k(chunk)

    for step in range(READY, n_fold):
        fetch(step, 0)
    for step in range(NEXT):
        pass_on(step, 0)
    for chunk in range(chunks):

        def source_step(step, carry):
            if chunk:

                @pl.when(step + AHEAD < n_fold)
                def _():
                    fetch(step + AHEAD, chunk)

            @pl.when(step + NEXT < n_fold)
            def _():
                pass_on(step + NEXT, chunk)

            if chunk < chunks - 1:

                @pl.when(step + AHEAD >= n_fold)
                def _():
                    fetch(step + AHEAD - n_fold, chunk + 1)

                @pl.when(step + NEXT >= n_fold)
                def _():
                    pass_on(step + NEXT - n_fold, chunk + 1)

            multiply(step, chunk)
            return carry

        lax.fori_loop(0, n_fold, source_step, 0)

    settle(0)

    def finish(step, carry):
        block = flip(outer, step * 2 + 1, n_outer)
        over_z(block, block).wait_recv()
        far = decode(z_in[block], j_local, v_pack)
        for j in range(j_local):
            kept[0, j] += far[j]
        return carry

    lax.fori_loop(0, n_outer // 2, finish, 0)

    for i in range(n_i):
        for j in range(j_local):
            own = pl.ds(j, a_rows, stride=j_local)
            values = kept[0, j, i * a_rows:(i + 1) * a_rows]
            main_w[own, :] = values[:, :LANES]
            rest_w[own, :rest] = values[:, LANES:]
        values = jnp.concatenate([main_w[...], rest_w[:, :rest]], axis=1)
        labels = cj_ref[...] ^ i_labels[i]
        full = [
            jnp.where(labels == vir_line[:, q * v_pack:(q + 1) * v_pack], values, 0.0) for q in range(FOLDS)
        ]
        full = jnp.concatenate(full, axis=1).astype(out_ref.dtype)
        out_ref[i] = full.reshape(a_rows, j_local, vir_total)

    for chunk in range(chunks):
        if slabs_of[chunk] is not None:
            for step in range(n_pair - 1):
                to_pair(step, chunk).wait_send()

        def drain(source, carry):
            @pl.when(source != fold)
            def _():
                to_fold(source, chunk).wait_send()

            for step in range(1, n_y):
                over_y(source, step, chunk).wait_send()
            for step in range(n_y):
                over_core(source, step, chunk).wait_send()
            return carry

        lax.fori_loop(0, n_fold, drain, 0)

    def drain_sums(block, carry):
        over_x(block).wait_send()

        @pl.when(block != outer)
        def _():
            over_z(block, outer).wait_send()

        return carry

    lax.fori_loop(0, n_outer, drain_sums, 0)


def body(n_pair, n_fold, amplitudes, cycle_block, occ_sizes, vir_sizes, window_i, window_occ):
    c_local, occ_total, j_local, vir_total = cycle_block.shape
    n_i, k_local, a_rows, _ = amplitudes.shape
    v_pack = vir_total // FOLDS
    split = n_pair // n_i
    rows = a_rows // split
    group = LANES // (v_pack - LANES)
    slabs = -(-k_local // group) * (group + 1)
    depth = occ_total // FOLDS * c_local
    wide = -(-depth // LANES) * LANES
    n_y, n_outer = n_pair // 2, n_fold // 2
    count = n_pair * rows
    lanes = (j_local + -(-(j_local * (v_pack - LANES) + 1) // LANES)) * LANES
    spans = spans_of(occ_total // FOLDS, c_local)
    chunks = len(spans)
    most = max(span[1] for span in spans) if k_local * FOLDS == occ_total else k_local
    loads = 8
    sems = pltpu.SemaphoreType.DMA
    smem = pl.BlockSpec(memory_space=pltpu.SMEM)
    hbm = pl.BlockSpec(memory_space=pl.ANY)
    kind = amplitudes.dtype
    return pl.pallas_call(
        functools.partial(cycle_kernel, n_pair, n_fold),
        out_shape=jax.ShapeDtypeStruct((n_i, a_rows, j_local, vir_total), kind),
        in_specs=[smem] * 4 + [hbm] * 2,
        out_specs=pl.BlockSpec(memory_space=pltpu.VMEM),
        scratch_shapes=[
            pltpu.VMEM((occ_total, vir_total), jnp.int32),
            pltpu.VMEM((FOLDS, 1, depth), kind),
            pltpu.VMEM((c_local * j_local, 1), jnp.int32),
            pltpu.VMEM((n_pair, slabs, rows, LANES), kind),
            pltpu.VMEM((2, most, rows, vir_total), kind),
            pltpu.VMEM((n_pair, slabs, rows, LANES), kind),
            pltpu.VMEM((n_fold, rows, wide), kind),
            pltpu.VMEM((n_fold, n_pair, rows, wide), kind),
            pltpu.VMEM((j_local, occ_total // 4, 4 * c_local, v_pack), kind),
            pltpu.VMEM((2, c_local, loads, j_local, vir_total), kind),
            pltpu.VMEM((c_local * j_local, LANES), jnp.float32),
            pltpu.VMEM((c_local * j_local, LANES), jnp.float32),
            pltpu.VMEM((n_fold, j_local, count, v_pack), jnp.float32),
            pltpu.VMEM((2, j_local, count, v_pack), jnp.float32),
        ]
        + [pltpu.VMEM((n_outer, count, lanes), jnp.int16)] * 5
        + [
            sems, sems((2,)), sems((2,)), sems((n_pair, chunks)), sems((n_pair, chunks)),
            sems((n_fold, chunks)), sems((n_fold, chunks)),
            sems((n_fold, n_y, chunks)), sems((n_fold, n_y, chunks)),
            sems((n_fold, n_y, chunks)), sems((n_fold, n_y, chunks)),
            sems((n_outer,)), sems((n_outer,)), sems((n_outer,)), sems((n_outer,)), sems((n_outer,)),
        ],
        compiler_params=pltpu.CompilerParams(
            collective_id=0, has_side_effects=True, vmem_limit_bytes=60 << 20
        ),
    )(
        occ_sizes, vir_sizes, window_i, window_occ,
        amplitudes.reshape(n_i, k_local, split, rows, vir_total), cycle_block,
    )


def solution(mesh):
    sizes = mesh.shape["pair"], mesh.shape["fold"]
    placed = (P(None, "pair", "fold", None), P("fold", None, "pair", None), P(), P(), P(), P())

    def run(*args):
        return body(*sizes, *args)

    return jax.shard_map(
        run, mesh=mesh, in_specs=placed, out_specs=P(None, "fold", "pair", None), check_vma=False
    )
```

```python
import functools
import math

import jax
import jax.numpy as jnp
from jax import lax
from jax.experimental import pallas as pl
from jax.experimental.pallas import tpu as pltpu
from jax.sharding import PartitionSpec as P

LANES = 128
FOLDS = 4
EARLY = 1
LATE = 6
READY = 6
AHEAD = 3
NEXT = 1
STEPS = 32000.0
FINE = 8.0


def bounds_of(sizes_ref):
    ends, total = [], 0
    for g in range(sizes_ref.shape[0]):
        total = total + sizes_ref[g]
        ends.append(total)
    return ends


def label_of(positions, ends):
    return functools.reduce(jnp.add, [jnp.where(positions >= end, 1, 0) for end in ends])


def split_by(positions, count):
    whole = jnp.floor((positions.astype(jnp.float32) + 0.5) * (1.0 / count)).astype(jnp.int32)
    return whole, positions - whole * count


def column(count):
    return lax.broadcasted_iota(jnp.int32, (count, 1), 0)


def line(count):
    return lax.broadcasted_iota(jnp.int32, (1, count), 1)


def narrow(labels):
    return labels.astype(jnp.float32).astype(jnp.bfloat16)


def fold_columns(values, rows, lanes):
    v_pack = values.shape[1] // FOLDS
    total = jnp.zeros((values.shape[0], v_pack), values.dtype)
    for q in range(FOLDS):
        cut = slice(q * v_pack, (q + 1) * v_pack)
        total = jnp.where(rows == lanes[:, cut], values[:, cut], total)
    return total


def flip(index, bits, count):
    total, bit = 0, 1
    while bit < count:
        total = total + (index // bit + bits // bit) % 2 * bit
        bit *= 2
    return total


def encode(parts, out_ref):
    top = functools.reduce(jnp.maximum, [jnp.max(jnp.abs(part), axis=1, keepdims=True) for part in parts])
    code = jnp.ceil(jnp.log2(jnp.maximum(top, 1e-30)) * FINE)
    factor = STEPS * jnp.exp2(code * (-1.0 / FINE))
    scaled = [jnp.round(part * factor).astype(jnp.int32) for part in parts]
    rest = [part[:, LANES:] for part in scaled]
    spare = LANES - sum(part.shape[1] for part in rest)
    rest.append(jnp.broadcast_to(code.astype(jnp.int32), (code.shape[0], spare)))
    for j, part in enumerate(scaled):
        out_ref[:, j * LANES:(j + 1) * LANES] = part[:, :LANES].astype(jnp.int16)
    out_ref[:, len(parts) * LANES:] = jnp.concatenate(rest, axis=1).astype(jnp.int16)


def decode(packed, count, width):
    values = packed.astype(jnp.int32).astype(jnp.float32)
    code = values[:, -1:]
    values = values * (jnp.exp2(code * (1.0 / FINE)) / STEPS)
    rest = width - LANES
    return [
        jnp.concatenate(
            [
                values[:, j * LANES:(j + 1) * LANES],
                values[:, count * LANES + j * rest:count * LANES + (j + 1) * rest],
            ],
            axis=1,
        )
        for j in range(count)
    ]


def spans_of(k_pack, c_local):
    step = LANES // math.gcd(LANES, c_local)
    return [(0, step), (step, k_pack - step)]


def cycle_kernel(
    n_pair, n_fold, occ_sizes, vir_sizes, window_i, window_occ, t_hbm, w_hbm, out_ref,
    occ_wide, col_ref, cj_ref, parts, raw_t, moved, wide, held, packed_w, raw_w, main_w, rest_w,
    total, kept, x_out, x_in, z_out, z_in, m_in,
    copy_sem, t_sem, w_sem, a_send, a_recv, f_send, f_recv, y_send, y_recv, c_send, c_recv,
    x_send, x_recv, z_send, z_recv, m_recv,
):
    pair, fold = lax.axis_index("pair"), lax.axis_index("fold")
    n_y, n_outer, here = n_pair // 2, n_fold // 2, n_fold // FOLDS
    y, core = pair // 2, pair % 2
    outer, half = fold // 2, fold % 2
    mate = y * 2 + 1 - core
    c_local, occ_total, j_local, vir_total = w_hbm.shape
    n_i, _, split, rows, _ = t_hbm.shape
    a_rows, v_pack = split * rows, vir_total // FOLDS
    k_pack, k_local = occ_total // FOLDS, occ_total // n_pair
    rest = v_pack - LANES
    group = LANES // rest
    spans = spans_of(k_pack, c_local)
    chunks = len(spans)
    lanes_of = [
        (first * c_local, -(-count * c_local // LANES) * LANES) for first, count in spans
    ]
    slabs = moved.shape[1]
    taken = spans if k_local == k_pack else [(0, k_local)] + [None] * (chunks - 1)
    slabs_of = [
        span and (span[0] // group * (group + 1), -(-span[1] // group) * (group + 1)) for span in taken
    ]

    occ_ends, vir_ends = bounds_of(occ_sizes), bounds_of(vir_sizes)
    i_labels = [label_of(window_i[i], occ_ends) for i in range(n_i)]
    j_labels = [label_of(window_occ[pair * j_local + j], occ_ends) for j in range(j_local)]
    vir_line = label_of(line(vir_total), vir_ends)

    def load_t(step, chunk):
        target = turn(step)
        first, count = taken[chunk]
        slot = step % 2
        return pltpu.make_async_copy(
            t_hbm.at[target // split, pl.ds(first, count), target % split],
            raw_t.at[slot, pl.ds(0, count)], t_sem.at[slot],
        )

    def turn(step):
        return (y + 1 + step // 2) % n_y * 2 + (core + 1 + step) % 2

    def to_pair(step, chunk):
        other = turn(step)
        first, count = slabs_of[chunk]
        return pltpu.make_async_remote_copy(
            src_ref=parts.at[other, pl.ds(first, count)],
            dst_ref=moved.at[pair, pl.ds(first, count)],
            send_sem=a_send.at[other, chunk], recv_sem=a_recv.at[pair, chunk],
            device_id={"pair": other},
        )

    def from_pair(step, chunk):
        other = turn(step)
        first, count = slabs_of[chunk]
        return pltpu.make_async_remote_copy(
            src_ref=parts.at[other, pl.ds(first, count)],
            dst_ref=moved.at[other, pl.ds(first, count)],
            send_sem=a_send.at[other, chunk], recv_sem=a_recv.at[other, chunk],
            device_id={"pair": other},
        )

    def piece_of(ref, index, chunk):
        return ref.at[(*index, slice(None), pl.ds(*lanes_of[chunk]))]

    def to_fold(target, chunk):
        return pltpu.make_async_remote_copy(
            src_ref=piece_of(wide, (target,), chunk), dst_ref=piece_of(held, (fold, pair), chunk),
            send_sem=f_send.at[target, chunk], recv_sem=f_recv.at[fold, chunk],
            device_id={"fold": target},
        )

    def from_fold(source, chunk):
        return pltpu.make_async_remote_copy(
            src_ref=piece_of(wide, (source,), chunk), dst_ref=piece_of(held, (source, pair), chunk),
            send_sem=f_send.at[source, chunk], recv_sem=f_recv.at[source, chunk],
            device_id={"fold": source},
        )

    def shared(source, other, whose, sends, recvs, mark, chunk, target):
        slot = piece_of(held, (source, whose), chunk)
        return pltpu.make_async_remote_copy(
            src_ref=slot, dst_ref=slot,
            send_sem=sends.at[source, other, chunk], recv_sem=recvs.at[source, mark, chunk],
            device_id={"pair": target},
        )

    def over_y(source, step, chunk):
        other = (y + step) % n_y
        return shared(source, other, pair, y_send, y_recv, y, chunk, other * 2 + core)

    def from_y(source, step, chunk):
        other = (y + step) % n_y
        target = other * 2 + core
        return shared(source, other, target, y_send, y_recv, other, chunk, target)

    def over_core(source, step, chunk):
        other = (y + step) % n_y
        return shared(source, other, other * 2 + core, c_send, c_recv, other, chunk, mate)

    def from_core(source, step, chunk):
        other = (y + step) % n_y
        return shared(source, other, other * 2 + 1 - core, c_send, c_recv, other, chunk, mate)

    def over_x(block):
        return pltpu.make_async_remote_copy(
            src_ref=x_out.at[block], dst_ref=x_in.at[block],
            send_sem=x_send.at[block], recv_sem=x_recv.at[block],
            device_id={"fold": outer * 2 + 1 - half},
        )

    def over_z(block, slot):
        return pltpu.make_async_remote_copy(
            src_ref=z_out.at[block], dst_ref=z_in.at[slot],
            send_sem=z_send.at[block], recv_sem=z_recv.at[slot],
            device_id={"fold": block * 2 + half},
        )

    def to_near(block):
        return pltpu.make_async_remote_copy(
            src_ref=z_out.at[block], dst_ref=m_in.at[block],
            send_sem=z_send.at[block], recv_sem=m_recv.at[block],
            device_id={"fold": flip(outer, 1, n_outer) * 2 + half},
        )

    def own_parts(chunk):
        first, count = slabs_of[chunk]
        return pltpu.make_async_copy(
            parts.at[pair, pl.ds(first, count)], moved.at[pair, pl.ds(first, count)], copy_sem
        )

    def pack_t(chunk):
        first, count = taken[chunk]

        def one(step, carry):
            target = turn(step)
            load_t(step, chunk).wait()
            slot = step % 2
            own_rows = narrow(
                label_of(fold * a_rows + target % split * rows + column(rows), vir_ends)
            )
            i_label = label_of(window_i[target // split], occ_ends)
            tails = []
            for k in range(first, first + count):
                lanes = narrow(vir_line ^ occ_wide[pl.ds(pair * k_local + k, 1), :] ^ i_label)
                chosen = fold_columns(raw_t[slot, k - first], own_rows, lanes)
                base = k // group * (group + 1)
                parts[target, base + k % group] = chosen[:, :LANES]
                tails.append(chosen[:, LANES:])
                if k == k_local - 1:
                    tails += [jnp.zeros_like(tails[0])] * (group - len(tails))
                if len(tails) == group:
                    parts[target, base + group] = jnp.concatenate(tails, axis=1)
                    tails = []

            @pl.when(step < n_pair - 1)
            def _():
                to_pair(step, chunk).start()

            @pl.when(step + 2 < n_pair)
            def _():
                load_t(step + 2, chunk).start()

            if chunk + 1 < chunks and taken[chunk + 1] is not None:

                @pl.when(step + 2 >= n_pair)
                def _():
                    load_t(step + 2 - n_pair, chunk + 1).start()

            return carry

        lax.fori_loop(0, n_pair, one, 0)
        own_parts(chunk).start()
        own_parts(chunk).wait()

    loads = raw_w.shape[2]
    n_loads = occ_total // loads

    def load_w(step):
        slot = step % 2
        return pltpu.make_async_copy(
            w_hbm.at[:, pl.ds(step * loads, loads)], raw_w.at[slot], w_sem.at[slot]
        )

    def pack_w(step, carry):
        load_w(step).wait()
        slot = step % 2
        for k in range(loads):
            lanes = narrow(vir_line ^ occ_wide[pl.ds(step * loads + k, 1), :])
            values = raw_w[slot, :, k].reshape(c_local * j_local, vir_total)
            chosen = fold_columns(values, narrow(cj_ref[...]), lanes).astype(jnp.float32)
            main_w[...] = chosen[:, :LANES]
            rest_w[:, :rest] = chosen[:, LANES:]
            block = step * (loads // 4) + k // 4
            place = slice(k % 4 * c_local, (k % 4 + 1) * c_local)
            for j in range(j_local):
                own = pl.ds(j, c_local, stride=j_local)
                packed_w[j, block, place, :LANES] = main_w[own, :].astype(packed_w.dtype)
                packed_w[j, block, place, LANES:] = rest_w[own, :][:, :rest].astype(packed_w.dtype)

        @pl.when(step + 2 < n_loads)
        def _():
            load_w(step + 2).start()

        return carry

    def block_of(step, chunk):
        return flip(outer, (step // 2 + (chunk == chunks - 1)) % n_outer, n_outer)

    def source_of(step, chunk):
        return block_of(step, chunk) * 2 + (half + 1 + step) % 2

    def relay(source, chunk):
        for step in range(1, n_y):
            over_y(source, step, chunk).start()
        over_core(source, 0, chunk).start()

    def fetch(step, chunk):
        source = source_of(step, chunk)

        @pl.when((source != fold) if chunk == 0 else (source // 2 != outer))
        def _():
            from_fold(source, chunk).wait_recv()
            relay(source, chunk)


    def pass_on(step, chunk):
        source = source_of(step, chunk)
        for other in range(1, n_y):
            from_y(source, other, chunk).wait_recv()
            over_core(source, other, chunk).start()

    def pack_k(chunk):
        first, count = spans[chunk]
        start, width = lanes_of[chunk]
        if slabs_of[chunk] is not None:
            for step in range(n_pair - 1):
                from_pair(step, chunk).wait_recv()
        own_rows = label_of(fold * a_rows + pair % split * rows + column(rows), vir_ends)
        own_rows = own_rows ^ label_of(window_i[pair // split], occ_ends)

        def quarter(step, carry):
            q = flip(fold // here, step, FOLDS)
            labels = narrow(own_rows ^ label_of(q * v_pack + line(v_pack), vir_ends))
            pieces = [[] for _ in range(here)]
            for kappa in range(first, first + count):
                chosen = jnp.zeros((rows, v_pack), moved.dtype)
                for s in range(FOLDS):
                    k = s * k_pack + kappa
                    side, inner = k // k_local, k % k_local
                    base, tail = inner // group * (group + 1), inner % group * rest
                    piece = jnp.concatenate(
                        [moved[side, base + inner % group], moved[side, base + group][:, tail:tail + rest]],
                        axis=1,
                    )
                    chosen = jnp.where(labels == narrow(occ_wide[k:k + 1, :v_pack]), piece, chosen)
                for f in range(here):
                    pieces[f].append(chosen[:, f * c_local:(f + 1) * c_local])
            spare = width - count * c_local
            for f in range(here):
                if spare:
                    pieces[f].append(jnp.zeros((rows, spare), moved.dtype))
                wide[q * here + f, :, start:start + width] = jnp.concatenate(pieces[f], axis=1)
            for f in range(here):

                @pl.when(step * here + f > 0)
                def _():
                    to_fold(q * here + (fold + f) % here, chunk).start()

            return carry

        lax.fori_loop(0, FOLDS, quarter, 0)
        own = pltpu.make_async_copy(
            piece_of(wide, (fold,), chunk), piece_of(held, (fold, pair), chunk), copy_sem
        )
        own.start()
        own.wait()
        relay(fold, chunk)

    def multiply(step, chunk):
        source = source_of(step, chunk)
        block = block_of(step, chunk)
        first, count = spans[chunk]
        start, depth = first * c_local, count * c_local
        for other in range(n_y):
            from_core(source, other, chunk).wait_recv()
        left = jnp.concatenate([held[source, p, :, start:start + depth] for p in range(n_pair)], axis=0)
        own_rows = label_of(source * a_rows + column(a_rows), vir_ends)
        labels = narrow(jnp.concatenate([own_rows ^ i_label for i_label in i_labels], axis=0))
        sums = [None] * j_local
        if chunk:
            sums = [total[source, j] for j in range(j_local)]
        for s in range(FOLDS):
            part = jnp.where(labels == col_ref[s, :, start:start + depth], left, jnp.zeros_like(left))
            place = (s * k_pack + first) // 4
            for j in range(j_local):
                right = packed_w[j, place:place + count // 4].reshape(depth, v_pack)
                term = jnp.dot(part, right, preferred_element_type=jnp.float32)
                sums[j] = term if sums[j] is None else sums[j] + term
        for j in range(j_local):
            total[source, j] = sums[j]
        if chunk < chunks - 1:
            return

        @pl.when(step % 2 == 0)
        def _():
            encode([total[source, j] for j in range(j_local)], x_out.at[block])
            over_x(block).start()

        @pl.when((step % 2 == 1) & (step > 1))
        def _():
            settle(step // 2)

    def settle(turned):
        block = flip(outer, turned, n_outer)
        over_x(block).wait_recv()
        near = decode(x_in[block], j_local, v_pack)
        near = [total[block * 2 + half, j] + near[j] for j in range(j_local)]
        late = 0 if isinstance(turned, int) else 1
        for j in range(j_local):
            kept[late, j] = near[j]

        @pl.when((turned % 2 == 1) & (turned > 1))
        def _():
            to_near(block).wait_recv()
            more = decode(m_in[block], j_local, v_pack)
            for j in range(j_local):
                kept[1, j] += more[j]

        @pl.when(turned > 0)
        def _():
            encode([kept[1, j] for j in range(j_local)], z_out.at[block])

        @pl.when((turned % 2 == 0) & (turned > 0))
        def _():
            to_near(block).start()

        @pl.when(turned % 2 == 1)
        def _():
            over_z(block, outer).start()

    load_t(0, 0).start()
    load_t(1, 0).start()
    load_w(0).start()
    load_w(1).start()
    barrier = pltpu.get_barrier_semaphore()
    for step in range(1, n_fold):
        pl.semaphore_signal(barrier, device_id={"fold": (fold + step) % n_fold})
    for step in range(1, n_pair):
        pl.semaphore_signal(barrier, device_id={"pair": (pair + step) % n_pair})

    occ_wide[...] = label_of(lax.broadcasted_iota(jnp.int32, (occ_total, vir_total), 0), occ_ends)
    pl.semaphore_wait(barrier, n_fold + n_pair - 2)
    for chunk in range(chunks):
        if taken[chunk] is not None:
            pack_t(chunk)
    c_of, j_of = split_by(column(c_local * j_local), j_local)
    j_mixed = functools.reduce(jnp.add, [jnp.where(j_of == j, j_labels[j], 0) for j in range(j_local)])
    cj_ref[...] = label_of(fold * c_local + c_of, vir_ends) ^ j_mixed
    kappa_of, c_of = split_by(line(k_pack * c_local), c_local)
    c_mixed = label_of(fold * c_local + c_of, vir_ends)
    for s in range(FOLDS):
        col_ref[s] = narrow(label_of(s * k_pack + kappa_of, occ_ends) ^ c_mixed)
    lax.fori_loop(0, EARLY, pack_w, 0)
    pack_k(0)

    def pack_w_relaying(step, carry):
        pack_w(step, carry)

        @pl.when((step > EARLY) & (step <= EARLY + READY))
        def _():
            fetch(step - EARLY - 1, 0)

        return carry

    lax.fori_loop(EARLY, LATE, pack_w_relaying, 0)
    for chunk in range(1, chunks):
        pack_k(chunk)
    lax.fori_loop(LATE, n_loads, pack_w_relaying, 0)

    for step in range(READY, n_fold):
        fetch(step, 0)
    for chunk in range(1, chunks):
        beside = outer * 2 + 1 - half
        from_fold(beside, chunk).wait_recv()
        relay(beside, chunk)
    for step in range(NEXT):
        pass_on(step, 0)
    for chunk in range(chunks):

        def source_step(step, carry):
            if chunk:

                @pl.when(step + AHEAD < n_fold)
                def _():
                    fetch(step + AHEAD, chunk)

            @pl.when(step + NEXT < n_fold)
            def _():
                pass_on(step + NEXT, chunk)

            if chunk < chunks - 1:

                @pl.when(step + AHEAD >= n_fold)
                def _():
                    fetch(step + AHEAD - n_fold, chunk + 1)

                @pl.when(step + NEXT >= n_fold)
                def _():
                    pass_on(step + NEXT - n_fold, chunk + 1)

            multiply(step, chunk)
            return carry

        lax.fori_loop(0, n_fold, source_step, 0)

    settle(0)

    def finish(step, carry):
        block = flip(outer, step * 2 + 1, n_outer)
        over_z(block, block).wait_recv()
        far = decode(z_in[block], j_local, v_pack)
        for j in range(j_local):
            kept[0, j] += far[j]
        return carry

    lax.fori_loop(0, n_outer // 2, finish, 0)

    for i in range(n_i):
        for j in range(j_local):
            own = pl.ds(j, a_rows, stride=j_local)
            values = kept[0, j, i * a_rows:(i + 1) * a_rows]
            main_w[own, :] = values[:, :LANES]
            rest_w[own, :rest] = values[:, LANES:]
        values = jnp.concatenate([main_w[...], rest_w[:, :rest]], axis=1)
        labels = cj_ref[...] ^ i_labels[i]
        full = [
            jnp.where(labels == vir_line[:, q * v_pack:(q + 1) * v_pack], values, 0.0) for q in range(FOLDS)
        ]
        full = jnp.concatenate(full, axis=1).astype(out_ref.dtype)
        out_ref[i] = full.reshape(a_rows, j_local, vir_total)

    for chunk in range(chunks):
        if slabs_of[chunk] is not None:
            for step in range(n_pair - 1):
                to_pair(step, chunk).wait_send()

        def drain(source, carry):
            @pl.when(source != fold)
            def _():
                to_fold(source, chunk).wait_send()

            for step in range(1, n_y):
                over_y(source, step, chunk).wait_send()
            for step in range(n_y):
                over_core(source, step, chunk).wait_send()
            return carry

        lax.fori_loop(0, n_fold, drain, 0)

    def drain_sums(block, carry):
        over_x(block).wait_send()

        @pl.when(block != outer)
        def _():
            over_z(block, outer).wait_send()

        return carry

    lax.fori_loop(0, n_outer, drain_sums, 0)


def body(n_pair, n_fold, amplitudes, cycle_block, occ_sizes, vir_sizes, window_i, window_occ):
    c_local, occ_total, j_local, vir_total = cycle_block.shape
    n_i, k_local, a_rows, _ = amplitudes.shape
    v_pack = vir_total // FOLDS
    split = n_pair // n_i
    rows = a_rows // split
    group = LANES // (v_pack - LANES)
    slabs = -(-k_local // group) * (group + 1)
    depth = occ_total // FOLDS * c_local
    wide = -(-depth // LANES) * LANES
    n_y, n_outer = n_pair // 2, n_fold // 2
    count = n_pair * rows
    lanes = (j_local + -(-(j_local * (v_pack - LANES) + 1) // LANES)) * LANES
    spans = spans_of(occ_total // FOLDS, c_local)
    chunks = len(spans)
    most = max(span[1] for span in spans) if k_local * FOLDS == occ_total else k_local
    loads = 8
    sems = pltpu.SemaphoreType.DMA
    smem = pl.BlockSpec(memory_space=pltpu.SMEM)
    hbm = pl.BlockSpec(memory_space=pl.ANY)
    kind = amplitudes.dtype
    return pl.pallas_call(
        functools.partial(cycle_kernel, n_pair, n_fold),
        out_shape=jax.ShapeDtypeStruct((n_i, a_rows, j_local, vir_total), kind),
        in_specs=[smem] * 4 + [hbm] * 2,
        out_specs=pl.BlockSpec(memory_space=pltpu.VMEM),
        scratch_shapes=[
            pltpu.VMEM((occ_total, vir_total), jnp.int32),
            pltpu.VMEM((FOLDS, 1, depth), kind),
            pltpu.VMEM((c_local * j_local, 1), jnp.int32),
            pltpu.VMEM((n_pair, slabs, rows, LANES), kind),
            pltpu.VMEM((2, most, rows, vir_total), kind),
            pltpu.VMEM((n_pair, slabs, rows, LANES), kind),
            pltpu.VMEM((n_fold, rows, wide), kind),
            pltpu.VMEM((n_fold, n_pair, rows, wide), kind),
            pltpu.VMEM((j_local, occ_total // 4, 4 * c_local, v_pack), kind),
            pltpu.VMEM((2, c_local, loads, j_local, vir_total), kind),
            pltpu.VMEM((c_local * j_local, LANES), jnp.float32),
            pltpu.VMEM((c_local * j_local, LANES), jnp.float32),
            pltpu.VMEM((n_fold, j_local, count, v_pack), jnp.float32),
            pltpu.VMEM((2, j_local, count, v_pack), jnp.float32),
        ]
        + [pltpu.VMEM((n_outer, count, lanes), jnp.int16)] * 5
        + [
            sems, sems((2,)), sems((2,)), sems((n_pair, chunks)), sems((n_pair, chunks)),
            sems((n_fold, chunks)), sems((n_fold, chunks)),
            sems((n_fold, n_y, chunks)), sems((n_fold, n_y, chunks)),
            sems((n_fold, n_y, chunks)), sems((n_fold, n_y, chunks)),
            sems((n_outer,)), sems((n_outer,)), sems((n_outer,)), sems((n_outer,)), sems((n_outer,)),
        ],
        compiler_params=pltpu.CompilerParams(
            collective_id=0, has_side_effects=True, vmem_limit_bytes=60 << 20
        ),
    )(
        occ_sizes, vir_sizes, window_i, window_occ,
        amplitudes.reshape(n_i, k_local, split, rows, vir_total), cycle_block,
    )


def solution(mesh):
    sizes = mesh.shape["pair"], mesh.shape["fold"]
    placed = (P(None, "pair", "fold", None), P("fold", None, "pair", None), P(), P(), P(), P())

    def run(*args):
        return body(*sizes, *args)

    return jax.shard_map(
        run, mesh=mesh, in_specs=placed, out_specs=P(None, "fold", "pair", None), check_vma=False
    )
```

```python
import functools
import math

import jax
import jax.numpy as jnp
from jax import lax
from jax.experimental import pallas as pl
from jax.experimental.pallas import tpu as pltpu
from jax.sharding import PartitionSpec as P

LANES = 128
FOLDS = 4
EARLY = 1
LATE = 6
READY = 6
AHEAD = 3
NEXT = 1
STEPS = 32000.0
FINE = 8.0


def bounds_of(sizes_ref):
    ends, total = [], 0
    for g in range(sizes_ref.shape[0]):
        total = total + sizes_ref[g]
        ends.append(total)
    return ends


def label_of(positions, ends):
    return functools.reduce(jnp.add, [jnp.where(positions >= end, 1, 0) for end in ends])


def split_by(positions, count):
    whole = jnp.floor((positions.astype(jnp.float32) + 0.5) * (1.0 / count)).astype(jnp.int32)
    return whole, positions - whole * count


def column(count):
    return lax.broadcasted_iota(jnp.int32, (count, 1), 0)


def line(count):
    return lax.broadcasted_iota(jnp.int32, (1, count), 1)


def narrow(labels):
    return labels.astype(jnp.float32).astype(jnp.bfloat16)


def fold_columns(values, rows, lanes):
    v_pack = values.shape[1] // FOLDS
    total = jnp.zeros((values.shape[0], v_pack), values.dtype)
    for q in range(FOLDS):
        cut = slice(q * v_pack, (q + 1) * v_pack)
        total = jnp.where(rows == lanes[:, cut], values[:, cut], total)
    return total


def flip(index, bits, count):
    total, bit = 0, 1
    while bit < count:
        total = total + (index // bit + bits // bit) % 2 * bit
        bit *= 2
    return total


def encode(parts, out_ref):
    top = functools.reduce(jnp.maximum, [jnp.max(jnp.abs(part), axis=1, keepdims=True) for part in parts])
    code = jnp.ceil(jnp.log2(jnp.maximum(top, 1e-30)) * FINE)
    factor = STEPS * jnp.exp2(code * (-1.0 / FINE))
    scaled = [jnp.round(part * factor).astype(jnp.int32) for part in parts]
    rest = [part[:, LANES:] for part in scaled]
    spare = LANES - sum(part.shape[1] for part in rest)
    rest.append(jnp.broadcast_to(code.astype(jnp.int32), (code.shape[0], spare)))
    for j, part in enumerate(scaled):
        out_ref[:, j * LANES:(j + 1) * LANES] = part[:, :LANES].astype(jnp.int16)
    out_ref[:, len(parts) * LANES:] = jnp.concatenate(rest, axis=1).astype(jnp.int16)


def decode(packed, count, width):
    values = packed.astype(jnp.int32).astype(jnp.float32)
    code = values[:, -1:]
    values = values * (jnp.exp2(code * (1.0 / FINE)) / STEPS)
    rest = width - LANES
    return [
        jnp.concatenate(
            [
                values[:, j * LANES:(j + 1) * LANES],
                values[:, count * LANES + j * rest:count * LANES + (j + 1) * rest],
            ],
            axis=1,
        )
        for j in range(count)
    ]


def spans_of(k_pack, c_local):
    step = LANES // math.gcd(LANES, c_local)
    return [(0, step), (step, k_pack - step)]


def cycle_kernel(
    n_pair, n_fold, occ_sizes, vir_sizes, window_i, window_occ, t_hbm, w_hbm, out_ref,
    occ_wide, col_ref, cj_ref, parts, raw_t, moved, wide, held, packed_w, raw_w, main_w, rest_w,
    total, kept, x_out, x_in, z_out, z_in, m_in,
    copy_sem, t_sem, w_sem, a_send, a_recv, f_send, f_recv, y_send, y_recv, c_send, c_recv,
    x_send, x_recv, z_send, z_recv, m_recv,
):
    pair, fold = lax.axis_index("pair"), lax.axis_index("fold")
    n_y, n_outer, here = n_pair // 2, n_fold // 2, n_fold // FOLDS
    y, core = pair // 2, pair % 2
    outer, half = fold // 2, fold % 2
    mate = y * 2 + 1 - core
    c_local, occ_total, j_local, vir_total = w_hbm.shape
    n_i, _, split, rows, _ = t_hbm.shape
    a_rows, v_pack = split * rows, vir_total // FOLDS
    k_pack, k_local = occ_total // FOLDS, occ_total // n_pair
    rest = v_pack - LANES
    group = LANES // rest
    spans = spans_of(k_pack, c_local)
    chunks = len(spans)
    lanes_of = [
        (first * c_local, -(-count * c_local // LANES) * LANES) for first, count in spans
    ]
    slabs = moved.shape[1]
    taken = spans if k_local == k_pack else [(0, k_local)] + [None] * (chunks - 1)
    slabs_of = [
        span and (span[0] // group * (group + 1), -(-span[1] // group) * (group + 1)) for span in taken
    ]

    occ_ends, vir_ends = bounds_of(occ_sizes), bounds_of(vir_sizes)
    i_labels = [label_of(window_i[i], occ_ends) for i in range(n_i)]
    j_labels = [label_of(window_occ[pair * j_local + j], occ_ends) for j in range(j_local)]
    vir_line = label_of(line(vir_total), vir_ends)

    def load_t(step, chunk):
        target = turn(step)
        first, count = taken[chunk]
        slot = step % 2
        return pltpu.make_async_copy(
            t_hbm.at[target // split, pl.ds(first, count), target % split],
            raw_t.at[slot, pl.ds(0, count)], t_sem.at[slot],
        )

    def turn(step):
        return (y + 1 + step // 2) % n_y * 2 + (core + 1 + step) % 2

    def to_pair(step, chunk):
        other = turn(step)
        first, count = slabs_of[chunk]
        return pltpu.make_async_remote_copy(
            src_ref=parts.at[other, pl.ds(first, count)],
            dst_ref=moved.at[pair, pl.ds(first, count)],
            send_sem=a_send.at[other, chunk], recv_sem=a_recv.at[pair, chunk],
            device_id={"pair": other},
        )

    def from_pair(step, chunk):
        other = turn(step)
        first, count = slabs_of[chunk]
        return pltpu.make_async_remote_copy(
            src_ref=parts.at[other, pl.ds(first, count)],
            dst_ref=moved.at[other, pl.ds(first, count)],
            send_sem=a_send.at[other, chunk], recv_sem=a_recv.at[other, chunk],
            device_id={"pair": other},
        )

    def piece_of(ref, index, chunk):
        return ref.at[(*index, slice(None), pl.ds(*lanes_of[chunk]))]

    def to_fold(target, chunk):
        return pltpu.make_async_remote_copy(
            src_ref=piece_of(wide, (target,), chunk), dst_ref=piece_of(held, (fold, pair), chunk),
            send_sem=f_send.at[target, chunk], recv_sem=f_recv.at[fold, chunk],
            device_id={"fold": target},
        )

    def from_fold(source, chunk):
        return pltpu.make_async_remote_copy(
            src_ref=piece_of(wide, (source,), chunk), dst_ref=piece_of(held, (source, pair), chunk),
            send_sem=f_send.at[source, chunk], recv_sem=f_recv.at[source, chunk],
            device_id={"fold": source},
        )

    def shared(source, other, whose, sends, recvs, mark, chunk, target):
        slot = piece_of(held, (source, whose), chunk)
        return pltpu.make_async_remote_copy(
            src_ref=slot, dst_ref=slot,
            send_sem=sends.at[source, other, chunk], recv_sem=recvs.at[source, mark, chunk],
            device_id={"pair": target},
        )

    def over_y(source, step, chunk):
        other = (y + step) % n_y
        return shared(source, other, pair, y_send, y_recv, y, chunk, other * 2 + core)

    def from_y(source, step, chunk):
        other = (y + step) % n_y
        target = other * 2 + core
        return shared(source, other, target, y_send, y_recv, other, chunk, target)

    def over_core(source, step, chunk):
        other = (y + step) % n_y
        return shared(source, other, other * 2 + core, c_send, c_recv, other, chunk, mate)

    def from_core(source, step, chunk):
        other = (y + step) % n_y
        return shared(source, other, other * 2 + 1 - core, c_send, c_recv, other, chunk, mate)

    def over_x(block):
        return pltpu.make_async_remote_copy(
            src_ref=x_out.at[block], dst_ref=x_in.at[block],
            send_sem=x_send.at[block], recv_sem=x_recv.at[block],
            device_id={"fold": outer * 2 + 1 - half},
        )

    def over_z(block, slot):
        return pltpu.make_async_remote_copy(
            src_ref=z_out.at[block], dst_ref=z_in.at[slot],
            send_sem=z_send.at[block], recv_sem=z_recv.at[slot],
            device_id={"fold": block * 2 + half},
        )

    def to_near(block):
        return pltpu.make_async_remote_copy(
            src_ref=z_out.at[block], dst_ref=m_in.at[block],
            send_sem=z_send.at[block], recv_sem=m_recv.at[block],
            device_id={"fold": flip(outer, 1, n_outer) * 2 + half},
        )

    def own_parts(chunk):
        first, count = slabs_of[chunk]
        return pltpu.make_async_copy(
            parts.at[pair, pl.ds(first, count)], moved.at[pair, pl.ds(first, count)], copy_sem
        )

    def pack_t(chunk):
        first, count = taken[chunk]

        def one(step, carry):
            target = turn(step)
            load_t(step, chunk).wait()
            slot = step % 2
            own_rows = narrow(
                label_of(fold * a_rows + target % split * rows + column(rows), vir_ends)
            )
            i_label = label_of(window_i[target // split], occ_ends)
            tails = []
            for k in range(first, first + count):
                lanes = narrow(vir_line ^ occ_wide[pl.ds(pair * k_local + k, 1), :] ^ i_label)
                chosen = fold_columns(raw_t[slot, k - first], own_rows, lanes)
                base = k // group * (group + 1)
                parts[target, base + k % group] = chosen[:, :LANES]
                tails.append(chosen[:, LANES:])
                if k == k_local - 1:
                    tails += [jnp.zeros_like(tails[0])] * (group - len(tails))
                if len(tails) == group:
                    parts[target, base + group] = jnp.concatenate(tails, axis=1)
                    tails = []

            @pl.when(step < n_pair - 1)
            def _():
                to_pair(step, chunk).start()

            @pl.when(step + 2 < n_pair)
            def _():
                load_t(step + 2, chunk).start()

            if chunk + 1 < chunks and taken[chunk + 1] is not None:

                @pl.when(step + 2 >= n_pair)
                def _():
                    load_t(step + 2 - n_pair, chunk + 1).start()

            return carry

        lax.fori_loop(0, n_pair, one, 0)
        own_parts(chunk).start()
        own_parts(chunk).wait()

    loads = raw_w.shape[2]
    n_loads = occ_total // loads

    def load_w(step):
        slot = step % 2
        return pltpu.make_async_copy(
            w_hbm.at[:, pl.ds(step * loads, loads)], raw_w.at[slot], w_sem.at[slot]
        )

    def pack_w(step, carry):
        load_w(step).wait()
        slot = step % 2
        for k in range(loads):
            lanes = narrow(vir_line ^ occ_wide[pl.ds(step * loads + k, 1), :])
            values = raw_w[slot, :, k].reshape(c_local * j_local, vir_total)
            chosen = fold_columns(values, narrow(cj_ref[...]), lanes).astype(jnp.float32)
            main_w[...] = chosen[:, :LANES]
            rest_w[:, :rest] = chosen[:, LANES:]
            block = step * (loads // 4) + k // 4
            place = slice(k % 4 * c_local, (k % 4 + 1) * c_local)
            for j in range(j_local):
                own = pl.ds(j, c_local, stride=j_local)
                packed_w[j, block, place, :LANES] = main_w[own, :].astype(packed_w.dtype)
                packed_w[j, block, place, LANES:] = rest_w[own, :][:, :rest].astype(packed_w.dtype)

        @pl.when(step + 2 < n_loads)
        def _():
            load_w(step + 2).start()

        return carry

    def block_of(step, chunk):
        return flip(outer, (step // 2 + (chunk == chunks - 1)) % n_outer, n_outer)

    def source_of(step, chunk):
        return block_of(step, chunk) * 2 + (half + 1 + step) % 2

    def relay(source, chunk):
        for step in range(1, n_y):
            over_y(source, step, chunk).start()
        over_core(source, 0, chunk).start()

    def fetch(step, chunk):
        source = source_of(step, chunk)

        @pl.when((source != fold) if chunk == 0 else (source // 2 != outer))
        def _():
            from_fold(source, chunk).wait_recv()
            relay(source, chunk)


    def pass_on(step, chunk):
        source = source_of(step, chunk)
        for other in range(1, n_y):
            from_y(source, other, chunk).wait_recv()
            over_core(source, other, chunk).start()

    def pack_k(chunk):
        first, count = spans[chunk]
        start, width = lanes_of[chunk]
        if slabs_of[chunk] is not None:
            for step in range(n_pair - 1):
                from_pair(step, chunk).wait_recv()
        own_rows = label_of(fold * a_rows + pair % split * rows + column(rows), vir_ends)
        own_rows = own_rows ^ label_of(window_i[pair // split], occ_ends)

        def quarter(step, carry):
            q = flip(fold // here, step, FOLDS)
            labels = narrow(own_rows ^ label_of(q * v_pack + line(v_pack), vir_ends))
            pieces = [[] for _ in range(here)]
            for kappa in range(first, first + count):
                chosen = jnp.zeros((rows, v_pack), moved.dtype)
                for s in range(FOLDS):
                    k = s * k_pack + kappa
                    side, inner = k // k_local, k % k_local
                    base, tail = inner // group * (group + 1), inner % group * rest
                    piece = jnp.concatenate(
                        [moved[side, base + inner % group], moved[side, base + group][:, tail:tail + rest]],
                        axis=1,
                    )
                    chosen = jnp.where(labels == narrow(occ_wide[k:k + 1, :v_pack]), piece, chosen)
                for f in range(here):
                    pieces[f].append(chosen[:, f * c_local:(f + 1) * c_local])
            spare = width - count * c_local
            for f in range(here):
                if spare:
                    pieces[f].append(jnp.zeros((rows, spare), moved.dtype))
                wide[q * here + f, :, start:start + width] = jnp.concatenate(pieces[f], axis=1)
            for f in range(here):

                @pl.when(step * here + f > 0)
                def _():
                    to_fold(q * here + (fold + f) % here, chunk).start()

            return carry

        lax.fori_loop(0, FOLDS, quarter, 0)
        own = pltpu.make_async_copy(
            piece_of(wide, (fold,), chunk), piece_of(held, (fold, pair), chunk), copy_sem
        )
        own.start()
        own.wait()
        relay(fold, chunk)

    def multiply(step, chunk):
        source = source_of(step, chunk)
        block = block_of(step, chunk)
        first, count = spans[chunk]
        start, depth = first * c_local, count * c_local
        if chunk == chunks - 1:

            @pl.when((step % 2 == 1) & (step > 1))
            def _():
                settle(step // 2)

        for other in range(n_y):
            from_core(source, other, chunk).wait_recv()
        left = jnp.concatenate([held[source, p, :, start:start + depth] for p in range(n_pair)], axis=0)
        own_rows = label_of(source * a_rows + column(a_rows), vir_ends)
        labels = narrow(jnp.concatenate([own_rows ^ i_label for i_label in i_labels], axis=0))
        sums = [None] * j_local
        if chunk:
            sums = [total[source, j] for j in range(j_local)]
        for s in range(FOLDS):
            part = jnp.where(labels == col_ref[s, :, start:start + depth], left, jnp.zeros_like(left))
            place = (s * k_pack + first) // 4
            for j in range(j_local):
                right = packed_w[j, place:place + count // 4].reshape(depth, v_pack)
                term = jnp.dot(part, right, preferred_element_type=jnp.float32)
                sums[j] = term if sums[j] is None else sums[j] + term
        for j in range(j_local):
            total[source, j] = sums[j]
        if chunk < chunks - 1:
            return

        @pl.when(step % 2 == 0)
        def _():
            encode([total[source, j] for j in range(j_local)], x_out.at[block])
            over_x(block).start()

    def settle(turned):
        block = flip(outer, turned, n_outer)
        over_x(block).wait_recv()
        near = decode(x_in[block], j_local, v_pack)
        near = [total[block * 2 + half, j] + near[j] for j in range(j_local)]
        late = 0 if isinstance(turned, int) else 1
        for j in range(j_local):
            kept[late, j] = near[j]

        @pl.when((turned % 2 == 1) & (turned > 1))
        def _():
            to_near(block).wait_recv()
            more = decode(m_in[block], j_local, v_pack)
            for j in range(j_local):
                kept[1, j] += more[j]

        @pl.when(turned > 0)
        def _():
            encode([kept[1, j] for j in range(j_local)], z_out.at[block])

        @pl.when((turned % 2 == 0) & (turned > 0))
        def _():
            to_near(block).start()

        @pl.when(turned % 2 == 1)
        def _():
            over_z(block, outer).start()

    load_t(0, 0).start()
    load_t(1, 0).start()
    load_w(0).start()
    load_w(1).start()
    barrier = pltpu.get_barrier_semaphore()
    for step in range(1, n_fold):
        pl.semaphore_signal(barrier, device_id={"fold": (fold + step) % n_fold})
    for step in range(1, n_pair):
        pl.semaphore_signal(barrier, device_id={"pair": (pair + step) % n_pair})

    occ_wide[...] = label_of(lax.broadcasted_iota(jnp.int32, (occ_total, vir_total), 0), occ_ends)
    pl.semaphore_wait(barrier, n_fold + n_pair - 2)
    for chunk in range(chunks):
        if taken[chunk] is not None:
            pack_t(chunk)
    c_of, j_of = split_by(column(c_local * j_local), j_local)
    j_mixed = functools.reduce(jnp.add, [jnp.where(j_of == j, j_labels[j], 0) for j in range(j_local)])
    cj_ref[...] = label_of(fold * c_local + c_of, vir_ends) ^ j_mixed
    kappa_of, c_of = split_by(line(k_pack * c_local), c_local)
    c_mixed = label_of(fold * c_local + c_of, vir_ends)
    for s in range(FOLDS):
        col_ref[s] = narrow(label_of(s * k_pack + kappa_of, occ_ends) ^ c_mixed)
    lax.fori_loop(0, EARLY, pack_w, 0)
    pack_k(0)

    def pack_w_relaying(step, carry):
        pack_w(step, carry)

        @pl.when((step > EARLY) & (step <= EARLY + READY))
        def _():
            fetch(step - EARLY - 1, 0)

        return carry

    lax.fori_loop(EARLY, LATE, pack_w_relaying, 0)
    for chunk in range(1, chunks):
        pack_k(chunk)
    lax.fori_loop(LATE, n_loads, pack_w_relaying, 0)

    for step in range(READY, n_fold):
        fetch(step, 0)
    for chunk in range(1, chunks):
        beside = outer * 2 + 1 - half
        from_fold(beside, chunk).wait_recv()
        relay(beside, chunk)
    for step in range(NEXT):
        pass_on(step, 0)
    for chunk in range(chunks):

        def source_step(step, carry):
            if chunk:

                @pl.when(step + AHEAD < n_fold)
                def _():
                    fetch(step + AHEAD, chunk)

            @pl.when(step + NEXT < n_fold)
            def _():
                pass_on(step + NEXT, chunk)

            if chunk < chunks - 1:

                @pl.when(step + AHEAD >= n_fold)
                def _():
                    fetch(step + AHEAD - n_fold, chunk + 1)

                @pl.when(step + NEXT >= n_fold)
                def _():
                    pass_on(step + NEXT - n_fold, chunk + 1)

            multiply(step, chunk)
            return carry

        lax.fori_loop(0, n_fold, source_step, 0)

    settle(0)

    def finish(step, carry):
        block = flip(outer, step * 2 + 1, n_outer)
        over_z(block, block).wait_recv()
        far = decode(z_in[block], j_local, v_pack)
        for j in range(j_local):
            kept[0, j] += far[j]
        return carry

    lax.fori_loop(0, n_outer // 2, finish, 0)

    for i in range(n_i):
        for j in range(j_local):
            own = pl.ds(j, a_rows, stride=j_local)
            values = kept[0, j, i * a_rows:(i + 1) * a_rows]
            main_w[own, :] = values[:, :LANES]
            rest_w[own, :rest] = values[:, LANES:]
        values = jnp.concatenate([main_w[...], rest_w[:, :rest]], axis=1)
        labels = cj_ref[...] ^ i_labels[i]
        full = [
            jnp.where(labels == vir_line[:, q * v_pack:(q + 1) * v_pack], values, 0.0) for q in range(FOLDS)
        ]
        full = jnp.concatenate(full, axis=1).astype(out_ref.dtype)
        out_ref[i] = full.reshape(a_rows, j_local, vir_total)

    for chunk in range(chunks):
        if slabs_of[chunk] is not None:
            for step in range(n_pair - 1):
                to_pair(step, chunk).wait_send()

        def drain(source, carry):
            @pl.when(source != fold)
            def _():
                to_fold(source, chunk).wait_send()

            for step in range(1, n_y):
                over_y(source, step, chunk).wait_send()
            for step in range(n_y):
                over_core(source, step, chunk).wait_send()
            return carry

        lax.fori_loop(0, n_fold, drain, 0)

    def drain_sums(block, carry):
        over_x(block).wait_send()

        @pl.when(block != outer)
        def _():
            over_z(block, outer).wait_send()

        return carry

    lax.fori_loop(0, n_outer, drain_sums, 0)


def body(n_pair, n_fold, amplitudes, cycle_block, occ_sizes, vir_sizes, window_i, window_occ):
    c_local, occ_total, j_local, vir_total = cycle_block.shape
    n_i, k_local, a_rows, _ = amplitudes.shape
    v_pack = vir_total // FOLDS
    split = n_pair // n_i
    rows = a_rows // split
    group = LANES // (v_pack - LANES)
    slabs = -(-k_local // group) * (group + 1)
    depth = occ_total // FOLDS * c_local
    wide = -(-depth // LANES) * LANES
    n_y, n_outer = n_pair // 2, n_fold // 2
    count = n_pair * rows
    lanes = (j_local + -(-(j_local * (v_pack - LANES) + 1) // LANES)) * LANES
    spans = spans_of(occ_total // FOLDS, c_local)
    chunks = len(spans)
    most = max(span[1] for span in spans) if k_local * FOLDS == occ_total else k_local
    loads = 8
    sems = pltpu.SemaphoreType.DMA
    smem = pl.BlockSpec(memory_space=pltpu.SMEM)
    hbm = pl.BlockSpec(memory_space=pl.ANY)
    kind = amplitudes.dtype
    return pl.pallas_call(
        functools.partial(cycle_kernel, n_pair, n_fold),
        out_shape=jax.ShapeDtypeStruct((n_i, a_rows, j_local, vir_total), kind),
        in_specs=[smem] * 4 + [hbm] * 2,
        out_specs=pl.BlockSpec(memory_space=pltpu.VMEM),
        scratch_shapes=[
            pltpu.VMEM((occ_total, vir_total), jnp.int32),
            pltpu.VMEM((FOLDS, 1, depth), kind),
            pltpu.VMEM((c_local * j_local, 1), jnp.int32),
            pltpu.VMEM((n_pair, slabs, rows, LANES), kind),
            pltpu.VMEM((2, most, rows, vir_total), kind),
            pltpu.VMEM((n_pair, slabs, rows, LANES), kind),
            pltpu.VMEM((n_fold, rows, wide), kind),
            pltpu.VMEM((n_fold, n_pair, rows, wide), kind),
            pltpu.VMEM((j_local, occ_total // 4, 4 * c_local, v_pack), kind),
            pltpu.VMEM((2, c_local, loads, j_local, vir_total), kind),
            pltpu.VMEM((c_local * j_local, LANES), jnp.float32),
            pltpu.VMEM((c_local * j_local, LANES), jnp.float32),
            pltpu.VMEM((n_fold, j_local, count, v_pack), jnp.float32),
            pltpu.VMEM((2, j_local, count, v_pack), jnp.float32),
        ]
        + [pltpu.VMEM((n_outer, count, lanes), jnp.int16)] * 5
        + [
            sems, sems((2,)), sems((2,)), sems((n_pair, chunks)), sems((n_pair, chunks)),
            sems((n_fold, chunks)), sems((n_fold, chunks)),
            sems((n_fold, n_y, chunks)), sems((n_fold, n_y, chunks)),
            sems((n_fold, n_y, chunks)), sems((n_fold, n_y, chunks)),
            sems((n_outer,)), sems((n_outer,)), sems((n_outer,)), sems((n_outer,)), sems((n_outer,)),
        ],
        compiler_params=pltpu.CompilerParams(
            collective_id=0, has_side_effects=True, vmem_limit_bytes=60 << 20
        ),
    )(
        occ_sizes, vir_sizes, window_i, window_occ,
        amplitudes.reshape(n_i, k_local, split, rows, vir_total), cycle_block,
    )


def solution(mesh):
    sizes = mesh.shape["pair"], mesh.shape["fold"]
    placed = (P(None, "pair", "fold", None), P("fold", None, "pair", None), P(), P(), P(), P())

    def run(*args):
        return body(*sizes, *args)

    return jax.shard_map(
        run, mesh=mesh, in_specs=placed, out_specs=P(None, "fold", "pair", None), check_vma=False
    )
```

```python
import functools
import math

import jax
import jax.numpy as jnp
from jax import lax
from jax.experimental import pallas as pl
from jax.experimental.pallas import tpu as pltpu
from jax.sharding import PartitionSpec as P

LANES = 128
FOLDS = 4
EARLY = 1
LATE = 6
READY = 8
AHEAD = 3
NEXT = 1
STEPS = 32000.0
FINE = 8.0


def bounds_of(sizes_ref):
    ends, total = [], 0
    for g in range(sizes_ref.shape[0]):
        total = total + sizes_ref[g]
        ends.append(total)
    return ends


def label_of(positions, ends):
    return functools.reduce(jnp.add, [jnp.where(positions >= end, 1, 0) for end in ends])


def split_by(positions, count):
    whole = jnp.floor((positions.astype(jnp.float32) + 0.5) * (1.0 / count)).astype(jnp.int32)
    return whole, positions - whole * count


def column(count):
    return lax.broadcasted_iota(jnp.int32, (count, 1), 0)


def line(count):
    return lax.broadcasted_iota(jnp.int32, (1, count), 1)


def narrow(labels):
    return labels.astype(jnp.float32).astype(jnp.bfloat16)


def fold_columns(values, rows, lanes):
    v_pack = values.shape[1] // FOLDS
    total = jnp.zeros((values.shape[0], v_pack), values.dtype)
    for q in range(FOLDS):
        cut = slice(q * v_pack, (q + 1) * v_pack)
        total = jnp.where(rows == lanes[:, cut], values[:, cut], total)
    return total


def flip(index, bits, count):
    total, bit = 0, 1
    while bit < count:
        total = total + (index // bit + bits // bit) % 2 * bit
        bit *= 2
    return total


def encode(parts, out_ref):
    top = functools.reduce(jnp.maximum, [jnp.max(jnp.abs(part), axis=1, keepdims=True) for part in parts])
    code = jnp.ceil(jnp.log2(jnp.maximum(top, 1e-30)) * FINE)
    factor = STEPS * jnp.exp2(code * (-1.0 / FINE))
    scaled = [jnp.round(part * factor).astype(jnp.int32) for part in parts]
    rest = [part[:, LANES:] for part in scaled]
    spare = LANES - sum(part.shape[1] for part in rest)
    rest.append(jnp.broadcast_to(code.astype(jnp.int32), (code.shape[0], spare)))
    for j, part in enumerate(scaled):
        out_ref[:, j * LANES:(j + 1) * LANES] = part[:, :LANES].astype(jnp.int16)
    out_ref[:, len(parts) * LANES:] = jnp.concatenate(rest, axis=1).astype(jnp.int16)


def decode(packed, count, width):
    values = packed.astype(jnp.int32).astype(jnp.float32)
    code = values[:, -1:]
    values = values * (jnp.exp2(code * (1.0 / FINE)) / STEPS)
    rest = width - LANES
    return [
        jnp.concatenate(
            [
                values[:, j * LANES:(j + 1) * LANES],
                values[:, count * LANES + j * rest:count * LANES + (j + 1) * rest],
            ],
            axis=1,
        )
        for j in range(count)
    ]


def spans_of(k_pack, c_local):
    step = LANES // math.gcd(LANES, c_local)
    return [(0, step), (step, k_pack - step)]


def cycle_kernel(
    n_pair, n_fold, occ_sizes, vir_sizes, window_i, window_occ, t_hbm, w_hbm, out_ref,
    occ_wide, col_ref, cj_ref, parts, raw_t, moved, wide, held, packed_w, raw_w, main_w, rest_w,
    total, kept, x_out, x_in, z_out, z_in, m_in,
    copy_sem, t_sem, w_sem, a_send, a_recv, f_send, f_recv, y_send, y_recv, c_send, c_recv,
    x_send, x_recv, z_send, z_recv, m_recv,
):
    pair, fold = lax.axis_index("pair"), lax.axis_index("fold")
    n_y, n_outer, here = n_pair // 2, n_fold // 2, n_fold // FOLDS
    y, core = pair // 2, pair % 2
    outer, half = fold // 2, fold % 2
    mate = y * 2 + 1 - core
    c_local, occ_total, j_local, vir_total = w_hbm.shape
    n_i, _, split, rows, _ = t_hbm.shape
    a_rows, v_pack = split * rows, vir_total // FOLDS
    k_pack, k_local = occ_total // FOLDS, occ_total // n_pair
    rest = v_pack - LANES
    group = LANES // rest
    spans = spans_of(k_pack, c_local)
    chunks = len(spans)
    lanes_of = [
        (first * c_local, -(-count * c_local // LANES) * LANES) for first, count in spans
    ]
    slabs = moved.shape[1]
    taken = spans if k_local == k_pack else [(0, k_local)] + [None] * (chunks - 1)
    slabs_of = [
        span and (span[0] // group * (group + 1), -(-span[1] // group) * (group + 1)) for span in taken
    ]

    occ_ends, vir_ends = bounds_of(occ_sizes), bounds_of(vir_sizes)
    i_labels = [label_of(window_i[i], occ_ends) for i in range(n_i)]
    j_labels = [label_of(window_occ[pair * j_local + j], occ_ends) for j in range(j_local)]
    vir_line = label_of(line(vir_total), vir_ends)

    def load_t(step, chunk):
        target = turn(step)
        first, count = taken[chunk]
        slot = step % 2
        return pltpu.make_async_copy(
            t_hbm.at[target // split, pl.ds(first, count), target % split],
            raw_t.at[slot, pl.ds(0, count)], t_sem.at[slot],
        )

    def turn(step):
        return (y + 1 + step // 2) % n_y * 2 + (core + 1 + step) % 2

    def to_pair(step, chunk):
        other = turn(step)
        first, count = slabs_of[chunk]
        return pltpu.make_async_remote_copy(
            src_ref=parts.at[other, pl.ds(first, count)],
            dst_ref=moved.at[pair, pl.ds(first, count)],
            send_sem=a_send.at[other, chunk], recv_sem=a_recv.at[pair, chunk],
            device_id={"pair": other},
        )

    def from_pair(step, chunk):
        other = turn(step)
        first, count = slabs_of[chunk]
        return pltpu.make_async_remote_copy(
            src_ref=parts.at[other, pl.ds(first, count)],
            dst_ref=moved.at[other, pl.ds(first, count)],
            send_sem=a_send.at[other, chunk], recv_sem=a_recv.at[other, chunk],
            device_id={"pair": other},
        )

    def piece_of(ref, index, chunk):
        return ref.at[(*index, slice(None), pl.ds(*lanes_of[chunk]))]

    def to_fold(target, chunk):
        return pltpu.make_async_remote_copy(
            src_ref=piece_of(wide, (target,), chunk), dst_ref=piece_of(held, (fold, pair), chunk),
            send_sem=f_send.at[target, chunk], recv_sem=f_recv.at[fold, chunk],
            device_id={"fold": target},
        )

    def from_fold(source, chunk):
        return pltpu.make_async_remote_copy(
            src_ref=piece_of(wide, (source,), chunk), dst_ref=piece_of(held, (source, pair), chunk),
            send_sem=f_send.at[source, chunk], recv_sem=f_recv.at[source, chunk],
            device_id={"fold": source},
        )

    def shared(source, other, whose, sends, recvs, mark, chunk, target):
        slot = piece_of(held, (source, whose), chunk)
        return pltpu.make_async_remote_copy(
            src_ref=slot, dst_ref=slot,
            send_sem=sends.at[source, other, chunk], recv_sem=recvs.at[source, mark, chunk],
            device_id={"pair": target},
        )

    def over_y(source, step, chunk):
        other = (y + step) % n_y
        return shared(source, other, pair, y_send, y_recv, y, chunk, other * 2 + core)

    def from_y(source, step, chunk):
        other = (y + step) % n_y
        target = other * 2 + core
        return shared(source, other, target, y_send, y_recv, other, chunk, target)

    def over_core(source, step, chunk):
        other = (y + step) % n_y
        return shared(source, other, other * 2 + core, c_send, c_recv, other, chunk, mate)

    def from_core(source, step, chunk):
        other = (y + step) % n_y
        return shared(source, other, other * 2 + 1 - core, c_send, c_recv, other, chunk, mate)

    def over_x(block):
        return pltpu.make_async_remote_copy(
            src_ref=x_out.at[block], dst_ref=x_in.at[block],
            send_sem=x_send.at[block], recv_sem=x_recv.at[block],
            device_id={"fold": outer * 2 + 1 - half},
        )

    def over_z(block, slot):
        return pltpu.make_async_remote_copy(
            src_ref=z_out.at[block], dst_ref=z_in.at[slot],
            send_sem=z_send.at[block], recv_sem=z_recv.at[slot],
            device_id={"fold": block * 2 + half},
        )

    def to_near(block):
        return pltpu.make_async_remote_copy(
            src_ref=z_out.at[block], dst_ref=m_in.at[block],
            send_sem=z_send.at[block], recv_sem=m_recv.at[block],
            device_id={"fold": flip(outer, 1, n_outer) * 2 + half},
        )

    def own_parts(chunk):
        first, count = slabs_of[chunk]
        return pltpu.make_async_copy(
            parts.at[pair, pl.ds(first, count)], moved.at[pair, pl.ds(first, count)], copy_sem
        )

    def pack_t(chunk):
        first, count = taken[chunk]

        def one(step, carry):
            target = turn(step)
            load_t(step, chunk).wait()
            slot = step % 2
            own_rows = narrow(
                label_of(fold * a_rows + target % split * rows + column(rows), vir_ends)
            )
            i_label = label_of(window_i[target // split], occ_ends)
            tails = []
            for k in range(first, first + count):
                lanes = narrow(vir_line ^ occ_wide[pl.ds(pair * k_local + k, 1), :] ^ i_label)
                chosen = fold_columns(raw_t[slot, k - first], own_rows, lanes)
                base = k // group * (group + 1)
                parts[target, base + k % group] = chosen[:, :LANES]
                tails.append(chosen[:, LANES:])
                if k == k_local - 1:
                    tails += [jnp.zeros_like(tails[0])] * (group - len(tails))
                if len(tails) == group:
                    parts[target, base + group] = jnp.concatenate(tails, axis=1)
                    tails = []

            @pl.when(step < n_pair - 1)
            def _():
                to_pair(step, chunk).start()

            @pl.when(step + 2 < n_pair)
            def _():
                load_t(step + 2, chunk).start()

            if chunk + 1 < chunks and taken[chunk + 1] is not None:

                @pl.when(step + 2 >= n_pair)
                def _():
                    load_t(step + 2 - n_pair, chunk + 1).start()

            return carry

        lax.fori_loop(0, n_pair, one, 0)
        own_parts(chunk).start()
        own_parts(chunk).wait()

    loads = raw_w.shape[2]
    n_loads = occ_total // loads

    def load_w(step):
        slot = step % 2
        return pltpu.make_async_copy(
            w_hbm.at[:, pl.ds(step * loads, loads)], raw_w.at[slot], w_sem.at[slot]
        )

    def pack_w(step, carry):
        load_w(step).wait()
        slot = step % 2
        for k in range(loads):
            lanes = narrow(vir_line ^ occ_wide[pl.ds(step * loads + k, 1), :])
            values = raw_w[slot, :, k].reshape(c_local * j_local, vir_total)
            chosen = fold_columns(values, narrow(cj_ref[...]), lanes).astype(jnp.float32)
            main_w[...] = chosen[:, :LANES]
            rest_w[:, :rest] = chosen[:, LANES:]
            block = step * (loads // 4) + k // 4
            place = slice(k % 4 * c_local, (k % 4 + 1) * c_local)
            for j in range(j_local):
                own = pl.ds(j, c_local, stride=j_local)
                packed_w[j, block, place, :LANES] = main_w[own, :].astype(packed_w.dtype)
                packed_w[j, block, place, LANES:] = rest_w[own, :][:, :rest].astype(packed_w.dtype)

        @pl.when(step + 2 < n_loads)
        def _():
            load_w(step + 2).start()

        return carry

    def block_of(step, chunk):
        return flip(outer, (step // 2 + (chunk == chunks - 1)) % n_outer, n_outer)

    def source_of(step, chunk):
        return block_of(step, chunk) * 2 + (half + 1 + step) % 2

    def relay(source, chunk):
        for step in range(1, n_y):
            over_y(source, step, chunk).start()
        over_core(source, 0, chunk).start()

    def fetch(step, chunk):
        source = source_of(step, chunk)

        @pl.when((source != fold) if chunk == 0 else (source // 2 != outer))
        def _():
            from_fold(source, chunk).wait_recv()
            relay(source, chunk)


    def pass_on(step, chunk):
        source = source_of(step, chunk)
        for other in range(1, n_y):
            from_y(source, other, chunk).wait_recv()
            over_core(source, other, chunk).start()

    def pack_k(chunk):
        first, count = spans[chunk]
        start, width = lanes_of[chunk]
        if slabs_of[chunk] is not None:
            for step in range(n_pair - 1):
                from_pair(step, chunk).wait_recv()
        own_rows = label_of(fold * a_rows + pair % split * rows + column(rows), vir_ends)
        own_rows = own_rows ^ label_of(window_i[pair // split], occ_ends)

        def quarter(step, carry):
            q = flip(fold // here, step, FOLDS)
            labels = narrow(own_rows ^ label_of(q * v_pack + line(v_pack), vir_ends))
            pieces = [[] for _ in range(here)]
            for kappa in range(first, first + count):
                chosen = jnp.zeros((rows, v_pack), moved.dtype)
                for s in range(FOLDS):
                    k = s * k_pack + kappa
                    side, inner = k // k_local, k % k_local
                    base, tail = inner // group * (group + 1), inner % group * rest
                    piece = jnp.concatenate(
                        [moved[side, base + inner % group], moved[side, base + group][:, tail:tail + rest]],
                        axis=1,
                    )
                    chosen = jnp.where(labels == narrow(occ_wide[k:k + 1, :v_pack]), piece, chosen)
                for f in range(here):
                    pieces[f].append(chosen[:, f * c_local:(f + 1) * c_local])
            spare = width - count * c_local
            for f in range(here):
                if spare:
                    pieces[f].append(jnp.zeros((rows, spare), moved.dtype))
                wide[q * here + f, :, start:start + width] = jnp.concatenate(pieces[f], axis=1)
            for f in range(here):

                @pl.when(step * here + f > 0)
                def _():
                    to_fold(q * here + (fold + f) % here, chunk).start()

            return carry

        lax.fori_loop(0, FOLDS, quarter, 0)
        own = pltpu.make_async_copy(
            piece_of(wide, (fold,), chunk), piece_of(held, (fold, pair), chunk), copy_sem
        )
        own.start()
        own.wait()
        relay(fold, chunk)

    def multiply(step, chunk):
        source = source_of(step, chunk)
        block = block_of(step, chunk)
        first, count = spans[chunk]
        start, depth = first * c_local, count * c_local
        if chunk == chunks - 1:

            @pl.when((step % 2 == 1) & (step > 1))
            def _():
                settle(step // 2)

        for other in range(n_y):
            from_core(source, other, chunk).wait_recv()
        left = jnp.concatenate([held[source, p, :, start:start + depth] for p in range(n_pair)], axis=0)
        own_rows = label_of(source * a_rows + column(a_rows), vir_ends)
        labels = narrow(jnp.concatenate([own_rows ^ i_label for i_label in i_labels], axis=0))
        sums = [None] * j_local
        if chunk:
            sums = [total[source, j] for j in range(j_local)]
        for s in range(FOLDS):
            part = jnp.where(labels == col_ref[s, :, start:start + depth], left, jnp.zeros_like(left))
            place = (s * k_pack + first) // 4
            for j in range(j_local):
                right = packed_w[j, place:place + count // 4].reshape(depth, v_pack)
                term = jnp.dot(part, right, preferred_element_type=jnp.float32)
                sums[j] = term if sums[j] is None else sums[j] + term
        for j in range(j_local):
            total[source, j] = sums[j]
        if chunk < chunks - 1:
            return

        @pl.when(step % 2 == 0)
        def _():
            encode([total[source, j] for j in range(j_local)], x_out.at[block])
            over_x(block).start()

    def settle(turned):
        block = flip(outer, turned, n_outer)
        over_x(block).wait_recv()
        near = decode(x_in[block], j_local, v_pack)
        near = [total[block * 2 + half, j] + near[j] for j in range(j_local)]
        late = 0 if isinstance(turned, int) else 1
        for j in range(j_local):
            kept[late, j] = near[j]

        @pl.when((turned % 2 == 1) & (turned > 1))
        def _():
            to_near(block).wait_recv()
            more = decode(m_in[block], j_local, v_pack)
            for j in range(j_local):
                kept[1, j] += more[j]

        @pl.when(turned > 0)
        def _():
            encode([kept[1, j] for j in range(j_local)], z_out.at[block])

        @pl.when((turned % 2 == 0) & (turned > 0))
        def _():
            to_near(block).start()

        @pl.when(turned % 2 == 1)
        def _():
            over_z(block, outer).start()

    load_t(0, 0).start()
    load_t(1, 0).start()
    load_w(0).start()
    load_w(1).start()
    barrier = pltpu.get_barrier_semaphore()
    for step in range(1, n_fold):
        pl.semaphore_signal(barrier, device_id={"fold": (fold + step) % n_fold})
    for step in range(1, n_pair):
        pl.semaphore_signal(barrier, device_id={"pair": (pair + step) % n_pair})

    occ_wide[...] = label_of(lax.broadcasted_iota(jnp.int32, (occ_total, vir_total), 0), occ_ends)
    pl.semaphore_wait(barrier, n_fold + n_pair - 2)
    for chunk in range(chunks):
        if taken[chunk] is not None:
            pack_t(chunk)
    c_of, j_of = split_by(column(c_local * j_local), j_local)
    j_mixed = functools.reduce(jnp.add, [jnp.where(j_of == j, j_labels[j], 0) for j in range(j_local)])
    cj_ref[...] = label_of(fold * c_local + c_of, vir_ends) ^ j_mixed
    kappa_of, c_of = split_by(line(k_pack * c_local), c_local)
    c_mixed = label_of(fold * c_local + c_of, vir_ends)
    for s in range(FOLDS):
        col_ref[s] = narrow(label_of(s * k_pack + kappa_of, occ_ends) ^ c_mixed)
    lax.fori_loop(0, EARLY, pack_w, 0)
    pack_k(0)

    def pack_w_relaying(step, carry):
        pack_w(step, carry)

        @pl.when((step > EARLY) & (step <= EARLY + READY))
        def _():
            fetch(step - EARLY - 1, 0)

        return carry

    lax.fori_loop(EARLY, LATE, pack_w_relaying, 0)
    for chunk in range(1, chunks):
        pack_k(chunk)
    lax.fori_loop(LATE, n_loads, pack_w_relaying, 0)

    for step in range(READY, n_fold):
        fetch(step, 0)
    for chunk in range(1, chunks):
        beside = outer * 2 + 1 - half
        from_fold(beside, chunk).wait_recv()
        relay(beside, chunk)
    for step in range(NEXT):
        pass_on(step, 0)
    for chunk in range(chunks):

        def source_step(step, carry):
            if chunk:

                @pl.when(step + AHEAD < n_fold)
                def _():
                    fetch(step + AHEAD, chunk)

            @pl.when(step + NEXT < n_fold)
            def _():
                pass_on(step + NEXT, chunk)

            if chunk < chunks - 1:

                @pl.when(step + AHEAD >= n_fold)
                def _():
                    fetch(step + AHEAD - n_fold, chunk + 1)

                @pl.when(step + NEXT >= n_fold)
                def _():
                    pass_on(step + NEXT - n_fold, chunk + 1)

            multiply(step, chunk)
            return carry

        lax.fori_loop(0, n_fold, source_step, 0)

    settle(0)

    def finish(step, carry):
        block = flip(outer, step * 2 + 1, n_outer)
        over_z(block, block).wait_recv()
        far = decode(z_in[block], j_local, v_pack)
        for j in range(j_local):
            kept[0, j] += far[j]
        return carry

    lax.fori_loop(0, n_outer // 2, finish, 0)

    for i in range(n_i):
        for j in range(j_local):
            own = pl.ds(j, a_rows, stride=j_local)
            values = kept[0, j, i * a_rows:(i + 1) * a_rows]
            main_w[own, :] = values[:, :LANES]
            rest_w[own, :rest] = values[:, LANES:]
        values = jnp.concatenate([main_w[...], rest_w[:, :rest]], axis=1)
        labels = cj_ref[...] ^ i_labels[i]
        full = [
            jnp.where(labels == vir_line[:, q * v_pack:(q + 1) * v_pack], values, 0.0) for q in range(FOLDS)
        ]
        full = jnp.concatenate(full, axis=1).astype(out_ref.dtype)
        out_ref[i] = full.reshape(a_rows, j_local, vir_total)

    for chunk in range(chunks):
        if slabs_of[chunk] is not None:
            for step in range(n_pair - 1):
                to_pair(step, chunk).wait_send()

        def drain(source, carry):
            @pl.when(source != fold)
            def _():
                to_fold(source, chunk).wait_send()

            for step in range(1, n_y):
                over_y(source, step, chunk).wait_send()
            for step in range(n_y):
                over_core(source, step, chunk).wait_send()
            return carry

        lax.fori_loop(0, n_fold, drain, 0)

    def drain_sums(block, carry):
        over_x(block).wait_send()

        @pl.when(block != outer)
        def _():
            over_z(block, outer).wait_send()

        return carry

    lax.fori_loop(0, n_outer, drain_sums, 0)


def body(n_pair, n_fold, amplitudes, cycle_block, occ_sizes, vir_sizes, window_i, window_occ):
    c_local, occ_total, j_local, vir_total = cycle_block.shape
    n_i, k_local, a_rows, _ = amplitudes.shape
    v_pack = vir_total // FOLDS
    split = n_pair // n_i
    rows = a_rows // split
    group = LANES // (v_pack - LANES)
    slabs = -(-k_local // group) * (group + 1)
    depth = occ_total // FOLDS * c_local
    wide = -(-depth // LANES) * LANES
    n_y, n_outer = n_pair // 2, n_fold // 2
    count = n_pair * rows
    lanes = (j_local + -(-(j_local * (v_pack - LANES) + 1) // LANES)) * LANES
    spans = spans_of(occ_total // FOLDS, c_local)
    chunks = len(spans)
    most = max(span[1] for span in spans) if k_local * FOLDS == occ_total else k_local
    loads = 8
    sems = pltpu.SemaphoreType.DMA
    smem = pl.BlockSpec(memory_space=pltpu.SMEM)
    hbm = pl.BlockSpec(memory_space=pl.ANY)
    kind = amplitudes.dtype
    return pl.pallas_call(
        functools.partial(cycle_kernel, n_pair, n_fold),
        out_shape=jax.ShapeDtypeStruct((n_i, a_rows, j_local, vir_total), kind),
        in_specs=[smem] * 4 + [hbm] * 2,
        out_specs=pl.BlockSpec(memory_space=pltpu.VMEM),
        scratch_shapes=[
            pltpu.VMEM((occ_total, vir_total), jnp.int32),
            pltpu.VMEM((FOLDS, 1, depth), kind),
            pltpu.VMEM((c_local * j_local, 1), jnp.int32),
            pltpu.VMEM((n_pair, slabs, rows, LANES), kind),
            pltpu.VMEM((2, most, rows, vir_total), kind),
            pltpu.VMEM((n_pair, slabs, rows, LANES), kind),
            pltpu.VMEM((n_fold, rows, wide), kind),
            pltpu.VMEM((n_fold, n_pair, rows, wide), kind),
            pltpu.VMEM((j_local, occ_total // 4, 4 * c_local, v_pack), kind),
            pltpu.VMEM((2, c_local, loads, j_local, vir_total), kind),
            pltpu.VMEM((c_local * j_local, LANES), jnp.float32),
            pltpu.VMEM((c_local * j_local, LANES), jnp.float32),
            pltpu.VMEM((n_fold, j_local, count, v_pack), jnp.float32),
            pltpu.VMEM((2, j_local, count, v_pack), jnp.float32),
        ]
        + [pltpu.VMEM((n_outer, count, lanes), jnp.int16)] * 5
        + [
            sems, sems((2,)), sems((2,)), sems((n_pair, chunks)), sems((n_pair, chunks)),
            sems((n_fold, chunks)), sems((n_fold, chunks)),
            sems((n_fold, n_y, chunks)), sems((n_fold, n_y, chunks)),
            sems((n_fold, n_y, chunks)), sems((n_fold, n_y, chunks)),
            sems((n_outer,)), sems((n_outer,)), sems((n_outer,)), sems((n_outer,)), sems((n_outer,)),
        ],
        compiler_params=pltpu.CompilerParams(
            collective_id=0, has_side_effects=True, vmem_limit_bytes=60 << 20
        ),
    )(
        occ_sizes, vir_sizes, window_i, window_occ,
        amplitudes.reshape(n_i, k_local, split, rows, vir_total), cycle_block,
    )


def solution(mesh):
    sizes = mesh.shape["pair"], mesh.shape["fold"]
    placed = (P(None, "pair", "fold", None), P("fold", None, "pair", None), P(), P(), P(), P())

    def run(*args):
        return body(*sizes, *args)

    return jax.shard_map(
        run, mesh=mesh, in_specs=placed, out_specs=P(None, "fold", "pair", None), check_vma=False
    )
```
